32 devices in a mesh: tile: 4 (over z), chan: 4 (over y, x), tm: 2 (over core).
Axes of the slice: x: 2, y: 2, z: 4, core: 2. Of those that a mesh axis runs over, the one named last changes fastest.
Arguments:
- observed_values: bfloat16 [2, 65536, 128], P('tm', ('tile', 'chan')), may hold values from -6 to 6
- observed_tile: int32 [2, 65536, 1], P('tm', ('tile', 'chan')), may hold values from 0 to 3; in each aligned block of 4096 rows (0 to 4095, 4096 to 8191, ..., all dimensions but the last counted through in order) at most 2048 rows name the same one
- observed_cell: int32 [2, 65536], P('tm', ('tile', 'chan')), may hold values from 0 to 2047
- patch_weight: bfloat16 [4, 256, 256], P(None, None, 'chan'), may hold values from -0.1875 to 0.1875
- depth_weight: bfloat16 [9, 256], P(None, 'chan'), may hold values from -2 to 2
- owners: int32 [4, 4], replicated, may hold values from 0 to 3, as said below
Outputs:
- owned: bfloat16 [4, 2, 4, 64, 256], P('tile', 'tm', None, None, 'chan')
The draws below stay inside these ranges and needn't reach their ends.
Inputs may be any that keep to these rules, and one draw needn't show every extreme that they name: `observed_tile`: in the rows of one device at most 2048 name the same tile. owners[t, j] - t is the same modulo 4 for every t and differs between any two j, so every row and every column of owners is a permutation.
All inputs are finite; a program needn't handle non-finite values.
Results may differ from the reference program's by a relative error of at most 0.014.
Values may be sent and summed in bfloat16 or wider, within the bound.
A program may use at most 64 MiB of HBM per device.

```python
import math
import jax
import jax.numpy as jnp
import numpy as np

V = 128
LAT = 256
HS = 32
WS = 64
OBS_DEV = 4096
CELLS = 2048
CAP = 2048
OBS_ALL = 65536
CHANNELS = 256
HR = 8
PC = 64
N_TILE = 4
N_TM = 2


def draw_owners(key, part):
    shifts = jax.random.permutation(jax.random.fold_in(key, 17), N_TILE)
    sources = jnp.arange(N_TILE)[:, None]
    return ((sources + shifts[None, :]) % N_TILE).astype(jnp.int32)


def with_ends(entries, key, smallest, largest):
    longest = entries.shape.index(max(entries.shape))
    spots = []
    for shift in (0, 1):
        where = [jax.random.randint(jax.random.fold_in(key, axis), (), 0, length) for axis, length in enumerate(entries.shape)]
        where[longest] = (where[longest] + shift) % entries.shape[longest]
        spots.append(tuple(where))
    return entries.at[spots[0]].set(smallest).at[spots[1]].set(largest)


def steps_of(rng, extent, split, least, top_value):
    loudness = 1.0
    for dim, blocks in split:
        heights = jax.random.uniform(jax.random.fold_in(jax.random.fold_in(rng, 6), dim), (blocks,), jnp.float32, least / len(split), top_value / len(split))
        loudness = loudness * jnp.repeat(jnp.exp(heights), extent[dim] // blocks).reshape((-1,) + (1,) * (len(extent) - 1 - dim))
    return loudness


def routed_block(rng, own, number, rows, amount, top, bound, skew):
    order = jax.random.permutation(rng, amount)
    packed, usual = shares(amount, rows * top, bound, skew, True), shares(amount, rows * top, bound, skew, False)
    places = jnp.arange(amount)

    def named(tallies, rotation):
        used = int((tallies > 0).sum())
        fixed = max(1, used // 4)
        moved = fixed + (places - fixed + rotation * (used - fixed)) % max(1, amount - fixed)
        return jnp.zeros((amount,), jnp.int32).at[order[jnp.where(places < fixed, places, moved)]].set(jnp.asarray(tallies, jnp.int32))

    tallies = jnp.where(number % 4 == 0, named(packed, number // 4), named(usual, number - number // 4 - 1))
    mixed = jax.random.permutation(jax.random.fold_in(own, 3), amount)
    source_of, receiver = mixed[0:amount // 2 * 2:2], mixed[1:amount // 2 * 2:2]
    slack = jnp.minimum(tallies[source_of] - 1, bound - tallies[receiver]) // 2
    slack = jnp.where((source_of == order[0]) | (receiver == order[0]) | (tallies[receiver] == 0), 0, jnp.maximum(slack, 0))
    moved = jax.random.randint(jax.random.fold_in(own, 4), (amount // 2,), 0, 1 << 20) % (slack + 1)
    tallies = tallies.at[source_of].add(-moved).at[receiver].add(moved)
    labels = jnp.searchsorted(jnp.cumsum(tallies), jnp.arange(rows * top), side="right").astype(jnp.int32)
    table = labels.reshape(top, rows).T
    table = table[jax.random.permutation(jax.random.fold_in(own, 1), rows)]
    rotation = jax.random.randint(jax.random.fold_in(own, 2), (rows, 1), 0, top)
    return jnp.take_along_axis(table, (jnp.arange(top)[None, :] + rotation) % top, axis=1)


def shares(count, total, bound, lean, full):
    portions = [(1 << 20) // math.isqrt(rank ** lean) + 1 for rank in range(1, count + 1)]
    largest = bound if full else min(bound, max(-(-total // count), total * portions[0] // sum(portions)))
    least = 1 if total - largest >= count - 1 else 0
    given, spare = [largest] + [least] * (count - 1), total - largest - least * (count - 1)
    while spare > 0:
        movable = [i for i in range(1, count) if given[i] < largest] or [i for i in range(1, count) if given[i] < bound]
        pool, remaining = sum([portions[i] for i in movable]), spare
        for i in movable:
            more = min(bound - given[i], max(1, remaining * portions[i] // pool), spare)
            given[i] = given[i] + more
            spare = spare - more
    return np.array(given)


def normal_values(own_key, extent, deviation, most, cuts=(), dtype=jnp.bfloat16):
    values = deviation * jax.random.normal(own_key, extent, jnp.float32)
    if cuts:
        values = values * steps_of(own_key, extent, cuts, -0.22, 0.18)
    return jnp.clip(values, -most, most).astype(dtype)


def setup_inputs(seed: int = 0) -> dict:
    splits = jax.random.split(jax.random.key(seed), 7)
    observed_values = normal_values(splits[0], (N_TM, OBS_ALL, V), 1.0, 6.0, ((0, 2), (1, 16)))
    observed_tile_keys = jax.random.split(jax.random.fold_in(splits[1], 1), N_TM * OBS_ALL // OBS_DEV)
    observed_tile_turns = jax.random.permutation(jax.random.fold_in(splits[1], 3), N_TM * OBS_ALL // OBS_DEV)
    observed_tile = jax.vmap(lambda own, number: routed_block(jax.random.fold_in(splits[1], 2), own, number, OBS_DEV, N_TILE, 1, CAP, 2))(observed_tile_keys, observed_tile_turns).reshape((N_TM, OBS_ALL, 1))
    observed_cell = with_ends(jax.random.randint(splits[2], (N_TM, OBS_ALL), 0, CELLS), jax.random.fold_in(splits[2], 1), 0, CELLS - 1).astype(jnp.int32)
    patch_weight = normal_values(splits[3], (4, CHANNELS, LAT), (4 * CHANNELS) ** -0.5, 0.1875, ((2, 4),))
    depth_weight = normal_values(splits[4], (9, LAT), 9 ** -0.5, 2.0, ((1, 4),))
    owners = draw_owners(jax.random.fold_in(splits[6], 71), 0)
    return dict(observed_values=observed_values, observed_tile=observed_tile, observed_cell=observed_cell, patch_weight=patch_weight, depth_weight=depth_weight, owners=owners)


def reference(observed_values, observed_tile, observed_cell, patch_weight, depth_weight, owners):
    height = HS * N_TILE
    half_cols = WS // 2
    fields = []
    for slot in range(N_TM):
        target = (observed_tile[slot, :, 0] * CELLS + observed_cell[slot]).astype(jnp.int32)
        totals = jax.ops.segment_sum(observed_values[slot].astype(jnp.float32), target, num_segments=N_TILE * CELLS)
        counts = jax.ops.segment_sum(jnp.ones(target.shape, jnp.float32), target, num_segments=N_TILE * CELLS)
        means = (totals / jnp.maximum(counts, 1.0)[:, None]).astype(jnp.bfloat16)
        fields.append(means.reshape(height, WS, V))
    stacked = jnp.concatenate(fields, axis=2)
    encoded = jnp.zeros(((height // 2) * half_cols, LAT), jnp.float32)
    for tap_row in range(2):
        for tap_col in range(2):
            window = stacked[tap_row::2, tap_col::2, :].reshape(-1, CHANNELS)
            encoded = encoded + jnp.dot(window, patch_weight[tap_row * 2 + tap_col], preferred_element_type=jnp.float32)
    hidden = jax.nn.gelu(encoded).astype(jnp.bfloat16).reshape(height // 2, half_cols, LAT)
    widened = jnp.pad(hidden.astype(jnp.float32), ((2, 2), (2, 2), (0, 0)))
    depth = jnp.zeros((height // 2, half_cols, LAT), jnp.float32)
    for tap_row in range(3):
        for tap_col in range(3):
            shifted = widened[2 * tap_row:2 * tap_row + height // 2, 2 * tap_col:2 * tap_col + half_cols, :]
            depth = depth + shifted * depth_weight[tap_row * 3 + tap_col].astype(jnp.float32)
    latent = (hidden.astype(jnp.float32) + depth).astype(jnp.bfloat16)
    pieces = latent.reshape(N_TILE, N_TM, HR, half_cols, LAT).reshape(N_TILE, N_TM, N_TILE, PC, LAT)
    order = jnp.arange(N_TILE).astype(jnp.int32)
    chosen = jnp.sum(order[None, None, :] * (owners[:, None, :] == order[None, :, None]).astype(jnp.int32), axis=2).astype(jnp.int32)
    gathered = pieces[order[None, :], :, chosen.T]
    return jnp.transpose(gathered, (0, 2, 1, 3, 4))
```

```python
import functools
import jax
import jax.numpy as jnp
from jax import lax
from jax.experimental import pallas as pl
from jax.experimental.pallas import tpu as pltpu
from jax.sharding import PartitionSpec as P

V = 128
HS = 32
WS = 64


def padded(x, sides, width):
    for axis, dim in sides:
        devices, length = (lax.axis_size(axis), x.shape[dim])
        up = [(i, (i + 1) % devices) for i in range(devices - 1)]
        down = [(j, i) for i, j in up]
        last = lax.slice_in_dim(x, length - width, length, axis=dim)
        first = lax.slice_in_dim(x, 0, width, axis=dim)
        before = lax.ppermute(last, axis, up)
        after = lax.ppermute(first, axis, down)
        x = jnp.concatenate([before, x, after], axis=dim)
    return x


def pack_rows(values, destination, placed, tile_count, capacity):
    match = (destination[:, None] == lax.iota(jnp.int32, tile_count)[None, :]).astype(jnp.int32)
    earlier = jnp.cumsum(match, axis=0) - match
    position = jnp.sum(earlier * match, axis=1)
    slot_index = destination * capacity + position
    width = values.shape[1]
    sent_values = jnp.zeros((tile_count * capacity, width), jnp.bfloat16).at[slot_index].set(values)
    sent_cells = jnp.full((tile_count * capacity,), -1, jnp.int32).at[slot_index].set(placed)
    return (
        sent_values.reshape(tile_count, capacity, width),
        sent_cells.reshape(tile_count, capacity),
    )


def grid_block(arrived_values, arrived_cells, first_cell):
    cell_ids = first_cell + lax.iota(jnp.int32, 128)
    matches = cell_ids[:, None] == arrived_cells[None, :]
    totals = jnp.dot(
        matches.astype(jnp.bfloat16), arrived_values, preferred_element_type=jnp.float32
    )
    counts = jnp.sum(matches.astype(jnp.float32), axis=1)
    return (totals, counts)


def patch_rows(field, weight, row_start, row_count):
    slab = lax.dynamic_slice_in_dim(field, 2 * row_start, 2 * row_count, 0)
    depth_in = field.shape[2]
    result = jnp.zeros((row_count * (field.shape[1] // 2), weight.shape[2]), jnp.float32)
    for tap_row in range(2):
        for tap_col in range(2):
            window = slab[tap_row::2, tap_col::2, :].reshape(-1, depth_in)
            result = result + jnp.dot(
                window, weight[tap_row * 2 + tap_col], preferred_element_type=jnp.float32
            )
    return result.reshape(row_count, field.shape[1] // 2, weight.shape[2])


def local(observed_values, observed_tile, observed_cell, patch_weight, depth_weight, owners):
    tile_count = lax.axis_size("tile")
    slot_count = lax.axis_size("tm")
    values = observed_values[0]
    capacity = 2 * values.shape[0] // tile_count
    sent_values, sent_cells = pack_rows(
        values, observed_tile[0, :, 0], observed_cell[0], tile_count, capacity
    )
    arrived = (
        lax.all_to_all(sent_values, "tile", split_axis=0, concat_axis=0, tiled=True),
        lax.all_to_all(sent_cells, "tile", split_axis=0, concat_axis=0, tiled=True),
    )
    arrived_values = arrived[0].reshape(-1, V)
    arrived_cells = arrived[1].reshape(-1)
    cell_count = HS * WS
    firsts = jnp.arange(cell_count // 128, dtype=jnp.int32) * 128
    totals, counts = lax.map(
        lambda first_cell: grid_block(arrived_values, arrived_cells, first_cell), firsts
    )
    totals = totals.reshape(cell_count, V)
    counts = counts.reshape(cell_count)
    totals, counts = (
        lax.psum(totals.astype(jnp.bfloat16), "chan").astype(jnp.float32),
        lax.psum(counts.astype(jnp.bfloat16), "chan").astype(jnp.float32),
    )
    means = (totals / jnp.maximum(counts, 1.0)[:, None]).astype(jnp.bfloat16)
    means = means.reshape(HS, WS, V)
    out_rows = HS // (2 * slot_count)
    half_cols = WS // 2
    stacked = lax.all_gather(means, "tm", axis=2, tiled=True)
    encoded = patch_rows(stacked, patch_weight, lax.axis_index("tm") * out_rows, out_rows)
    hidden = jax.nn.gelu(encoded).astype(jnp.bfloat16)
    rimmed = padded(hidden, ((("tile", "tm"), 0),), 2)
    widened = jnp.pad(rimmed, ((0, 0), (2, 2), (0, 0))).astype(jnp.float32)
    depth = jnp.zeros(hidden.shape, jnp.float32)
    for tap_row in range(3):
        for tap_col in range(3):
            shifted = widened[
                2 * tap_row : 2 * tap_row + out_rows, 2 * tap_col : 2 * tap_col + half_cols, :
            ]
            depth = depth + shifted * depth_weight[tap_row * 3 + tap_col].astype(jnp.float32)
    latent = (hidden.astype(jnp.float32) + depth).astype(jnp.bfloat16)
    channels = latent.shape[2]
    pieces = latent.reshape(tile_count, -1, channels)
    own_row = lax.dynamic_index_in_dim(owners, lax.axis_index("tile"), 0, keepdims=False)
    order = lax.iota(jnp.int32, tile_count)
    chosen = jnp.sum(
        order[None, :] * (own_row[None, :] == order[:, None]).astype(jnp.int32), axis=1
    )
    outgoing = pieces[chosen]
    received = lax.all_to_all(outgoing, "tile", split_axis=0, concat_axis=0, tiled=True)
    return received.reshape(1, 1, tile_count, -1, channels)


def fused_kernel(
    values_hbm, column_hbm, tile_hbm, cell_hbm, weight_hbm, depth_hbm, owners_hbm, out_ref,
    values_ref, column_ref, tile_ref, cell_ref, depth_ref, owners_ref,
    masked, onehot, position, partial, first, second_src, second, third_src, third,
    count_src, count_in, weights, means, hidden_src, hidden_all,
    load_sems, send_sems, recv_sems, first_recv, second_recv, third_recv,
):
    f32, bf16 = jnp.float32, jnp.bfloat16
    n_tile, n_chan, n_core = (lax.axis_size(a) for a in ("tile", "chan", "tm"))
    me_t, me_c, me_s = (lax.axis_index(a) for a in ("tile", "chan", "tm"))
    rows, width = values_ref.shape
    block = partial.shape[3]
    quarter = block // 4
    half_cols = WS // 2
    flip_x = me_c + 1 - 2 * (me_c % 2)
    flip_y = (me_c + 2) % 4
    diagonal = 3 - me_c
    near = (flip_x, flip_y)
    far = (flip_y, flip_x)
    other = 1 - me_s
    shifts = (2, 1, 3, 0)
    own = n_tile - 1
    sends = {n: send_sems.at[i] for i, n in enumerate(SENDS)}
    recvs = {n: recv_sems.at[i] for i, n in enumerate(RECVS)}

    def remote(source, target, send, recv, device):
        return pltpu.make_async_remote_copy(
            src_ref=source, dst_ref=target, send_sem=send, recv_sem=recv,
            device_id=device, device_id_type=pl.DeviceIdType.MESH,
        )

    def all_of(ref, send, recv):
        return remote(ref, ref, send, recv, (me_t, me_c, other))

    offsets = [
        (a, b, c) for a in range(n_tile) for b in range(n_chan) for c in range(n_core)
    ][1:]
    offsets = sorted(offsets, key=lambda o: (2, 1, 3, 0).index(o[0]))

    def at(a, b, c):
        return ((me_t + a) % n_tile, (me_c + b) % n_chan, (me_s + c) % n_core)

    loads = [
        pltpu.make_async_copy(source, target, load_sems.at[i])
        for i, (source, target) in enumerate((
            (weight_hbm, weights.at[:, :, me_c]), (column_hbm, column_ref), (cell_hbm, cell_ref),
            (values_hbm, values_ref), (tile_hbm, tile_ref), (depth_hbm, depth_ref),
            (owners_hbm, owners_ref),
        ))
    ]
    for i in (2, 1, 3, 0, 4, 5, 6):
        loads[i].start()
    barrier = pltpu.get_barrier_semaphore()
    for offset in offsets:
        pl.semaphore_signal(
            barrier, inc=1, device_id=at(*offset), device_id_type=pl.DeviceIdType.MESH
        )

    def weight_copy(o):
        here = weights.at[me_s, :, me_c]
        return remote(
            here, here, sends["weight"], recvs["weight"], (me_t, (me_c + o) % n_chan, me_s)
        )

    def pass_copy(o):
        here = weights.at[me_s, :, (me_c - o + n_chan) % n_chan]
        return remote(here, here, sends["pass"], recvs["pass"], (me_t, me_c, other))

    def count_copy(a, b, c):
        to = at(a, b, c)
        return remote(
            count_src.at[(to[0] * n_chan + to[1]) * n_core + to[2]],
            count_in.at[(c * n_tile + a) * n_chan + b],
            sends["count"], recvs["count"], to,
        )

    def first_copy(h, k, q):
        return remote(
            partial.at[h, k, q], first.at[h, k, q],
            sends["first"], first_recv.at[k, q], (me_t, near[h], me_s),
        )

    def second_copy(h, q):
        return remote(
            second_src.at[h, q], second.at[h, q],
            sends["second"], second_recv.at[q], (me_t, far[h], me_s),
        )

    def third_copy(h, q):
        return remote(
            third_src.at[h, q], third.at[q, me_s], sends["third"], third_recv.at[q],
            ((me_t + shifts[q]) % n_tile, me_c, h),
        )

    loads[2].wait()
    cell = cell_ref[...]
    row, col = cell // WS, cell % WS
    position[...] = (
        (row // 4) * block + (row % 2) * (2 * quarter) + (col % 2) * quarter
        + ((row % 4) // 2) * half_cols + col // 2
    )
    loads[1].wait()
    columns = jnp.transpose(column_ref[...].astype(f32))
    loads[3].wait()

    def mask_rows(pair):
        for i in range(rows // 128):
            tiles = jnp.broadcast_to(columns[:, i:i + 1], (128, width))
            taken = values_ref[i * 128:(i + 1) * 128, :].astype(f32)
            for u in range(2):
                wanted = ((me_t + shifts[2 * pair + u]) % n_tile).astype(f32)
                masked[pair, i * 128:(i + 1) * 128, u * width:(u + 1) * width] = jnp.where(
                    tiles == wanted, taken, 0.0
                ).astype(bf16)

    ids = lax.broadcasted_iota(jnp.int32, (block, rows), 0)

    def grid_block(pair):
        def step(k, carry):
            if pair == 0:
                for h in range(2):
                    picks = (diagonal, near[h], far[h], me_c)
                    j = sum(jnp.where(k == i, p, 0) for i, p in enumerate(picks))
                    base = (h * n_chan + j) * block
                    onehot[k, h * block:(h + 1) * block] = (
                        ids == position[...] - base
                    ).astype(bf16)
            sums = jnp.dot(onehot[k], masked[pair], preferred_element_type=f32)
            for h in range(2):
                for u in range(2):
                    partial[h, k, 2 * pair + u] = sums[
                        h * block:(h + 1) * block, u * width:(u + 1) * width
                    ].astype(bf16)
            return carry
        return step

    def send_first(k, q):
        for h in range(2):
            first_copy(h, k, q).start()

    def send_second(q):
        all_of(first.at[:, 0, q], sends["first"], first_recv.at[0, q]).wait_recv()
        for h in range(2):
            second_src[h, q] = (
                partial[h, 2, q].astype(f32) + first[h, 0, q].astype(f32)
            ).astype(bf16)
            second_copy(h, q).start()

    def send_third(q):
        all_of(first.at[:, 1, q], sends["first"], first_recv.at[1, q]).wait_recv()
        all_of(second.at[:, q], sends["second"], second_recv.at[q]).wait_recv()
        for h in range(2):
            third_src[h, q] = (
                partial[h, 3, q].astype(f32) + first[h, 1, q].astype(f32)
                + second[h, q].astype(f32)
            ).astype(bf16)
            if q != own:
                third_copy(h, q).start()
        if q == own:
            third_copy_own.start()

    third_copy_own = remote(
        third_src.at[other, own], third.at[own, me_s], sends["third"], third_recv.at[own],
        (me_t, me_c, other),
    )

    mask_rows(0)
    lax.fori_loop(0, 2, grid_block(0), 0)
    pl.semaphore_wait(barrier, len(offsets))
    for k in range(2):
        for q in range(2):
            send_first(k, q)
    mask_rows(1)
    lax.fori_loop(2, 4, grid_block(0), 0)
    lax.fori_loop(0, 2, grid_block(1), 0)
    send_second(0)
    send_second(1)
    send_first(0, 2)
    send_first(1, 2)
    lax.fori_loop(2, 4, grid_block(1), 0)
    loads[4].wait()
    pos = position[...]
    inner = pos % block
    code = (tile_ref[...] * n_chan + (pos // block) % n_chan) * 4
    code = code + (pos // (block * n_chan)) * 2 + inner // 128
    code_ids = lax.broadcasted_iota(jnp.int32, (n_tile * n_chan * 4, rows), 0)
    lane_ids = lax.broadcasted_iota(jnp.int32, (128, rows), 0)
    counts = lax.dot_general(
        (code_ids == code).astype(bf16), (lane_ids == inner % 128).astype(bf16),
        (((1,), (1,)), ((), ())), preferred_element_type=f32,
    )
    count_src[...] = counts.reshape(n_tile * n_chan * n_core, 2, 128)
    send_third(0)
    send_third(1)
    send_second(2)
    send_first(0, 3)
    send_first(1, 3)
    loads[0].wait()
    for o in range(1, n_chan):
        weight_copy(o).start()
    send_third(2)
    send_second(3)
    for offset in offsets:
        count_copy(*offset).start()

    here = (me_t * n_core + me_s) * n_chan + me_c
    count = n_tile * n_core * n_chan
    hidden_all[0] = jnp.zeros((half_cols, 128), bf16)
    hidden_all[count + 1] = jnp.zeros((half_cols, 128), bf16)
    loads[5].wait()
    loads[6].wait()
    taps9 = depth_ref[...].astype(f32)
    taps9 = jnp.concatenate([taps9, taps9], axis=1)

    all_of(weights.at[0, :, 0:n_chan - 1], sends["weight"], recvs["weight"]).wait_recv()
    for o in range(1, n_chan):
        pass_copy(o).start()
    send_third(own)

    all_of(count_in.at[0:len(offsets)], sends["count"], recvs["count"]).wait_recv()
    mine = count_src[here_index(me_t, me_c, me_s, n_chan, n_core)]
    theirs = jnp.zeros(mine.shape, f32)
    for i in range(n_tile * n_chan):
        if i:
            mine = mine + count_in[i]
        theirs = theirs + count_in[n_tile * n_chan + i]

    for q in range(own):
        all_of(third.at[q], sends["third"], third_recv.at[q]).wait_recv()
    third_copy_own.wait_recv()
    for slot, counted in ((me_s, mine), (other, theirs)):
        summed = third[0, slot].astype(f32)
        for q in range(1, own):
            summed = summed + third[q, slot].astype(f32)
        if slot is me_s:
            summed = summed + third_src[me_s, own].astype(f32)
        else:
            summed = summed + third[own, slot].astype(f32)
        divisor = jnp.maximum(counted, 1.0)
        for u in range(block // 128):
            each = jnp.transpose(jnp.broadcast_to(divisor[u:u + 1, :], (128, 128)))
            means[slot, u * 128:(u + 1) * 128] = (summed[u * 128:(u + 1) * 128] / each).astype(bf16)

    all_of(weights.at[0, :, 0:n_chan - 1], sends["pass"], recvs["pass"]).wait_recv()
    lanes = weights.shape[3]
    encoded = jnp.zeros((quarter, n_chan * lanes), f32)
    for a in range(2):
        for b in range(2):
            at_row = (2 * a + b) * quarter
            fields = jnp.concatenate(
                [means[s, at_row:at_row + quarter] for s in range(n_core)], axis=1
            )
            encoded = encoded + lax.dot_general(
                fields, weights[a, b].reshape(n_chan * lanes, n_core * width),
                (((1,), (1,)), ((), ())), preferred_element_type=f32,
            )
    hidden = jax.nn.gelu(encoded)
    lane = lax.broadcasted_iota(jnp.int32, (half_cols, 128), 1)
    for g in range(n_chan // 2):
        upper = hidden[:half_cols, g * 128:(g + 1) * 128]
        lower = hidden[half_cols:, g * 128:(g + 1) * 128]
        hidden_src[2 * g] = jnp.where(lane < 64, upper, pltpu.roll(lower, 64, 1)).astype(bf16)
        hidden_src[2 * g + 1] = jnp.where(lane < 64, pltpu.roll(upper, 64, 1), lower).astype(bf16)

    def hidden_copy(i):
        to = at(*offsets[i])
        return remote(
            hidden_src.at[to[1]], hidden_all.at[here + 1], sends["hidden"], recvs["hidden"], to
        )

    on_edge = me_c % (n_chan - 1) == 0
    for i, (_, b, c) in enumerate(offsets):
        if c == 0:
            hidden_copy(i).start()

    @pl.when(on_edge)
    def _():
        for i, (_, b, c) in enumerate(offsets):
            if c:
                hidden_copy(i).start()

    hidden_all[here + 1] = hidden_src[me_c]
    all_of(first, sends["first"], first_recv.at[0, 0]).wait_send()
    all_of(second, sends["second"], second_recv.at[0]).wait_send()
    all_of(third.at[0:own], sends["third"], third_recv.at[0]).wait_send()
    all_of(third.at[own, 0], sends["third"], third_recv.at[own]).wait_send()
    all_of(weights.at[0, :, 0:n_chan - 1], sends["weight"], recvs["weight"]).wait_send()
    all_of(weights.at[0, :, 0:n_chan - 1], sends["pass"], recvs["pass"]).wait_send()
    all_of(count_in.at[0:len(offsets)], sends["count"], recvs["count"]).wait_send()
    every = n_tile * n_chan
    all_of(
        hidden_all.at[0:every - 1 + 2 * n_tile], sends["hidden"], recvs["hidden"]
    ).wait_recv()
    line = lax.broadcasted_iota(jnp.int32, (half_cols, 128), 0)
    for t in range(n_tile):
        j = jnp.int32(0)
        for i in range(n_chan):
            j = jnp.where(owners_ref[t, i] == me_t, i, j)
        at_piece = (t * n_core + me_s) * n_chan + j + 1
        total = jnp.zeros((half_cols, 128), f32)
        for p in range(3):
            field = hidden_all[at_piece + p - 1].astype(f32)
            before = jnp.where(line >= 2, pltpu.roll(field, 2, 0), 0.0)
            after = jnp.where(line < half_cols - 2, pltpu.roll(field, half_cols - 2, 0), 0.0)
            for q, shifted in enumerate((before, field, after)):
                total = total + shifted * taps9[3 * p + q:3 * p + q + 1, :]
            if p == 1:
                middle = field
        latent = middle + total
        out_ref[t, 0:half_cols] = latent[:, :64].astype(bf16)
        out_ref[t, half_cols:] = latent[:, 64:].astype(bf16)
    all_of(hidden_all.at[0:every - 1], sends["hidden"], recvs["hidden"]).wait_send()

    @pl.when(on_edge)
    def _():
        all_of(hidden_all.at[0:every], sends["hidden"], recvs["hidden"]).wait_send()


def here_index(t, c, s, n_chan, n_core):
    return (t * n_chan + c) * n_core + s


SENDS = ("first", "second", "third", "weight", "pass", "count", "hidden")
RECVS = ("weight", "pass", "count", "hidden")


def fused(observed_values, observed_tile, observed_cell, patch_weight, depth_weight, owners):
    f32, bf16, i32 = jnp.float32, jnp.bfloat16, jnp.int32
    n_tile, n_chan, n_core = (lax.axis_size(a) for a in ("tile", "chan", "tm"))
    values = observed_values[0]
    rows, width = values.shape
    depth_in, lanes = patch_weight.shape[1:]
    turned = jnp.swapaxes(patch_weight, 1, 2).reshape(2, 2, lanes, depth_in)
    block = HS * WS // (n_core * n_chan)
    cells = block // 4
    dma, vmem = pltpu.SemaphoreType.DMA, pltpu.VMEM
    pieces = n_tile * n_core * n_chan
    out = pl.pallas_call(
        fused_kernel,
        out_shape=jax.ShapeDtypeStruct((n_tile, cells, lanes), bf16),
        in_specs=[pl.BlockSpec(memory_space=pl.ANY)] * 7,
        out_specs=pl.BlockSpec(memory_space=pltpu.VMEM),
        scratch_shapes=[
            vmem((rows, width), bf16),
            vmem((rows // 128, 128), i32),
            vmem((1, rows), i32),
            vmem((1, rows), i32),
            vmem(depth_weight.shape, bf16),
            pltpu.SMEM(owners.shape, i32),
            vmem((2, rows, 2 * width), bf16),
            vmem((4, 2 * block, rows), bf16),
            vmem((1, rows), i32),
            vmem((2, 4, n_tile, block, width), bf16),
            vmem((2, 2, n_tile, block, width), bf16),
            vmem((2, n_tile, block, width), bf16),
            vmem((2, n_tile, block, width), bf16),
            vmem((2, n_tile, block, width), bf16),
            vmem((n_tile, 2, block, width), bf16),
            vmem((pieces, 2, 128), f32),
            vmem((pieces, 2, 128), f32),
            vmem((2, 2, n_chan, lanes, depth_in), bf16),
            vmem((2, block, width), bf16),
            vmem((n_chan, cells // 2, 128), bf16),
            vmem((pieces + 2, cells // 2, 128), bf16),
            dma((7,)), dma((len(SENDS),)), dma((len(RECVS),)),
            dma((2, n_tile)), dma((n_tile,)), dma((n_tile,)),
        ],
        compiler_params=pltpu.CompilerParams(
            collective_id=0, has_side_effects=True, vmem_limit_bytes=56 * 2**20
        ),
    )(
        values, observed_tile.reshape(rows // 128, 128), observed_tile.reshape(1, rows),
        observed_cell, turned, depth_weight, owners,
    )
    return out.reshape(1, 1, n_tile, cells, lanes)


def fits(mesh):
    tile, chan, tm = (mesh.shape[a] for a in ("tile", "chan", "tm"))
    return tile == 4 and chan == 4 and tm == 2


def solution(mesh):
    placed = (
        P("tm", ("tile", "chan"), None),
        P("tm", ("tile", "chan"), None),
        P("tm", ("tile", "chan")),
        P(None, None, "chan"),
        P(None, "chan"),
        P(),
    )
    return jax.shard_map(
        fused if fits(mesh) else local,
        mesh=mesh,
        in_specs=placed,
        out_specs=P("tile", "tm", None, None, "chan"),
        check_vma=False,
    )
```

```python
import functools
import jax
import jax.numpy as jnp
from jax import lax
from jax.experimental import pallas as pl
from jax.experimental.pallas import tpu as pltpu
from jax.sharding import PartitionSpec as P

V = 128
HS = 32
WS = 64


def padded(x, sides, width):
    for axis, dim in sides:
        devices, length = (lax.axis_size(axis), x.shape[dim])
        up = [(i, (i + 1) % devices) for i in range(devices - 1)]
        down = [(j, i) for i, j in up]
        last = lax.slice_in_dim(x, length - width, length, axis=dim)
        first = lax.slice_in_dim(x, 0, width, axis=dim)
        before = lax.ppermute(last, axis, up)
        after = lax.ppermute(first, axis, down)
        x = jnp.concatenate([before, x, after], axis=dim)
    return x


def pack_rows(values, destination, placed, tile_count, capacity):
    match = (destination[:, None] == lax.iota(jnp.int32, tile_count)[None, :]).astype(jnp.int32)
    earlier = jnp.cumsum(match, axis=0) - match
    position = jnp.sum(earlier * match, axis=1)
    slot_index = destination * capacity + position
    width = values.shape[1]
    sent_values = jnp.zeros((tile_count * capacity, width), jnp.bfloat16).at[slot_index].set(values)
    sent_cells = jnp.full((tile_count * capacity,), -1, jnp.int32).at[slot_index].set(placed)
    return (
        sent_values.reshape(tile_count, capacity, width),
        sent_cells.reshape(tile_count, capacity),
    )


def grid_block(arrived_values, arrived_cells, first_cell):
    cell_ids = first_cell + lax.iota(jnp.int32, 128)
    matches = cell_ids[:, None] == arrived_cells[None, :]
    totals = jnp.dot(
        matches.astype(jnp.bfloat16), arrived_values, preferred_element_type=jnp.float32
    )
    counts = jnp.sum(matches.astype(jnp.float32), axis=1)
    return (totals, counts)


def patch_rows(field, weight, row_start, row_count):
    slab = lax.dynamic_slice_in_dim(field, 2 * row_start, 2 * row_count, 0)
    depth_in = field.shape[2]
    result = jnp.zeros((row_count * (field.shape[1] // 2), weight.shape[2]), jnp.float32)
    for tap_row in range(2):
        for tap_col in range(2):
            window = slab[tap_row::2, tap_col::2, :].reshape(-1, depth_in)
            result = result + jnp.dot(
                window, weight[tap_row * 2 + tap_col], preferred_element_type=jnp.float32
            )
    return result.reshape(row_count, field.shape[1] // 2, weight.shape[2])


def local(observed_values, observed_tile, observed_cell, patch_weight, depth_weight, owners):
    tile_count = lax.axis_size("tile")
    slot_count = lax.axis_size("tm")
    values = observed_values[0]
    capacity = 2 * values.shape[0] // tile_count
    sent_values, sent_cells = pack_rows(
        values, observed_tile[0, :, 0], observed_cell[0], tile_count, capacity
    )
    arrived = (
        lax.all_to_all(sent_values, "tile", split_axis=0, concat_axis=0, tiled=True),
        lax.all_to_all(sent_cells, "tile", split_axis=0, concat_axis=0, tiled=True),
    )
    arrived_values = arrived[0].reshape(-1, V)
    arrived_cells = arrived[1].reshape(-1)
    cell_count = HS * WS
    firsts = jnp.arange(cell_count // 128, dtype=jnp.int32) * 128
    totals, counts = lax.map(
        lambda first_cell: grid_block(arrived_values, arrived_cells, first_cell), firsts
    )
    totals = totals.reshape(cell_count, V)
    counts = counts.reshape(cell_count)
    totals, counts = (
        lax.psum(totals.astype(jnp.bfloat16), "chan").astype(jnp.float32),
        lax.psum(counts.astype(jnp.bfloat16), "chan").astype(jnp.float32),
    )
    means = (totals / jnp.maximum(counts, 1.0)[:, None]).astype(jnp.bfloat16)
    means = means.reshape(HS, WS, V)
    out_rows = HS // (2 * slot_count)
    half_cols = WS // 2
    stacked = lax.all_gather(means, "tm", axis=2, tiled=True)
    encoded = patch_rows(stacked, patch_weight, lax.axis_index("tm") * out_rows, out_rows)
    hidden = jax.nn.gelu(encoded).astype(jnp.bfloat16)
    rimmed = padded(hidden, ((("tile", "tm"), 0),), 2)
    widened = jnp.pad(rimmed, ((0, 0), (2, 2), (0, 0))).astype(jnp.float32)
    depth = jnp.zeros(hidden.shape, jnp.float32)
    for tap_row in range(3):
        for tap_col in range(3):
            shifted = widened[
                2 * tap_row : 2 * tap_row + out_rows, 2 * tap_col : 2 * tap_col + half_cols, :
            ]
            depth = depth + shifted * depth_weight[tap_row * 3 + tap_col].astype(jnp.float32)
    latent = (hidden.astype(jnp.float32) + depth).astype(jnp.bfloat16)
    channels = latent.shape[2]
    pieces = latent.reshape(tile_count, -1, channels)
    own_row = lax.dynamic_index_in_dim(owners, lax.axis_index("tile"), 0, keepdims=False)
    order = lax.iota(jnp.int32, tile_count)
    chosen = jnp.sum(
        order[None, :] * (own_row[None, :] == order[:, None]).astype(jnp.int32), axis=1
    )
    outgoing = pieces[chosen]
    received = lax.all_to_all(outgoing, "tile", split_axis=0, concat_axis=0, tiled=True)
    return received.reshape(1, 1, tile_count, -1, channels)


def fused_kernel(
    values_hbm, column_hbm, tile_hbm, cell_hbm, weight_hbm, depth_hbm, owners_hbm, out_ref,
    values_ref, column_ref, tile_ref, cell_ref, depth_ref, owners_ref,
    masked_a, masked_b, onehot_a, onehot_b, onehot_c, onehot_d, position, partial, first, second_src, second, third_src, third,
    count_src, count_in, weights, means, hidden_src, hidden_all,
    load_sems, send_sems, recv_sems, first_recv, second_recv, third_recv, relays,
):
    f32, bf16 = jnp.float32, jnp.bfloat16
    n_tile, n_chan, n_core = (lax.axis_size(a) for a in ("tile", "chan", "tm"))
    me_t, me_c, me_s = (lax.axis_index(a) for a in ("tile", "chan", "tm"))
    rows, width = values_ref.shape
    block = partial.shape[3]
    quarter = block // 4
    half_cols = WS // 2
    flip_x = me_c + 1 - 2 * (me_c % 2)
    flip_y = (me_c + 2) % 4
    diagonal = 3 - me_c
    near = (flip_x, flip_y)
    far = (flip_y, flip_x)
    other = 1 - me_s
    masked = (masked_a, masked_b)
    onehot = (onehot_a, onehot_b, onehot_c, onehot_d)
    shifts = (2, 1, 3, 0)
    own = n_tile - 1
    sends = {n: send_sems.at[i] for i, n in enumerate(SENDS)}
    recvs = {n: recv_sems.at[i] for i, n in enumerate(RECVS)}

    def remote(source, target, send, recv, device):
        return pltpu.make_async_remote_copy(
            src_ref=source, dst_ref=target, send_sem=send, recv_sem=recv,
            device_id=device, device_id_type=pl.DeviceIdType.MESH,
        )

    def signal(sem, device):
        pl.semaphore_signal(sem, inc=1, device_id=device, device_id_type=pl.DeviceIdType.MESH)

    def all_of(ref, send, recv):
        return remote(ref, ref, send, recv, (me_t, me_c, other))

    offsets = [
        (a, b, c) for a in range(n_tile) for b in range(n_chan) for c in range(n_core)
    ][1:]
    offsets = sorted(offsets, key=lambda o: (2, 1, 3, 0).index(o[0]))

    def at(a, b, c):
        return ((me_t + a) % n_tile, (me_c + b) % n_chan, (me_s + c) % n_core)

    loads = [
        pltpu.make_async_copy(source, target, load_sems.at[i])
        for i, (source, target) in enumerate((
            (weight_hbm, weights.at[:, :, me_c]), (column_hbm, column_ref), (cell_hbm, cell_ref),
            (values_hbm, values_ref), (tile_hbm, tile_ref), (depth_hbm, depth_ref),
            (owners_hbm, owners_ref),
        ))
    ]
    for i in (2, 1, 3, 0, 4, 5, 6):
        loads[i].start()

    def signal_near(sem):
        for o in range(1, n_chan):
            signal(sem, (me_t, (me_c + o) % n_chan, me_s))
        signal(sem, (me_t, me_c, other))

        @pl.when(me_t > 0)
        def _():
            signal(sem, (me_t - 1, me_c, me_s))

        @pl.when(me_t < n_tile - 1)
        def _():
            signal(sem, (me_t + 1, me_c, me_s))

    def wait_near(sem):
        inner_tile = jnp.where((me_t > 0) & (me_t < n_tile - 1), 1, 0)
        pl.semaphore_wait(sem, n_chan + 1 + inner_tile)

    def relay(i):
        if i:
            wait_near(relays.at[i - 1])
        if i < RELAYS:
            signal_near(relays.at[i])

    barrier = pltpu.get_barrier_semaphore()
    signal_near(barrier)

    def weight_copy(o):
        here = weights.at[me_s, :, me_c]
        return remote(
            here, here, sends["weight"], recvs["weight"], (me_t, (me_c + o) % n_chan, me_s)
        )

    def pass_copy(o):
        here = weights.at[me_s, :, (me_c - o + n_chan) % n_chan]
        return remote(here, here, sends["pass"], recvs["pass"], (me_t, me_c, other))

    def count_copy(a, b, c):
        to = at(a, b, c)
        return remote(
            count_src.at[(to[0] * n_chan + to[1]) * n_core + to[2]],
            count_in.at[(c * n_tile + a) * n_chan + b],
            sends["count"], recvs["count"], to,
        )

    def first_copy(h, k, q):
        return remote(
            partial.at[h, k, q], first.at[h, k, q],
            sends["first"], first_recv.at[k, q], (me_t, near[h], me_s),
        )

    def second_copy(h, q):
        return remote(
            second_src.at[h, q], second.at[h, q],
            sends["second"], second_recv.at[q], (me_t, far[h], me_s),
        )

    def third_copy(h, q):
        return remote(
            third_src.at[h, q], third.at[q, me_s], sends["third"], third_recv.at[q],
            ((me_t + shifts[q]) % n_tile, me_c, h),
        )

    loads[2].wait()
    cell = cell_ref[...]
    row, col = cell // WS, cell % WS
    position[...] = (
        (row // 4) * block + (row % 2) * (2 * quarter) + (col % 2) * quarter
        + ((row % 4) // 2) * half_cols + col // 2
    )
    loads[0].wait()
    wait_near(barrier)
    for o in range(1, n_chan):
        weight_copy(o).start()
    relay(0)
    loads[1].wait()
    columns = jnp.transpose(column_ref[...].astype(f32))
    loads[3].wait()

    def mask_rows(pair):
        for i in range(rows // 128):
            tiles = jnp.broadcast_to(columns[:, i:i + 1], (128, width)).astype(bf16)
            taken = values_ref[i * 128:(i + 1) * 128, :]
            for u in range(2):
                wanted = ((me_t + shifts[2 * pair + u]) % n_tile).astype(f32).astype(bf16)
                masked[pair][i * 128:(i + 1) * 128, u * width:(u + 1) * width] = jnp.where(
                    tiles == wanted, taken, jnp.zeros_like(taken)
                )

    ids = lax.broadcasted_iota(jnp.int32, (block, rows), 0).astype(bf16)

    def mark(k):
        for h in range(2):
            j = (diagonal, near[h], far[h], me_c)[k]
            offset = (position[...] - (h * n_chan + j) * block).astype(bf16)
            onehot[k][h * block:(h + 1) * block] = jnp.where(
                ids == offset, jnp.ones((), bf16), jnp.zeros((), bf16)
            )

    def grid_block(k, pair):
        sums = [
            jnp.dot(
                onehot[k][h * block:(h + 1) * block], masked[pair][...],
                preferred_element_type=f32,
            )
            for h in range(2)
        ]
        for h in range(2):
            for u in range(2):
                partial[h, k, 2 * pair + u] = sums[h][:, u * width:(u + 1) * width].astype(bf16)

    def send_first(k, q):
        for h in range(2):
            first_copy(h, k, q).start()

    def send_second(q):
        all_of(first.at[:, 0, q], sends["first"], first_recv.at[0, q]).wait_recv()
        for h in range(2):
            second_src[h, q] = (
                partial[h, 2, q].astype(f32) + first[h, 0, q].astype(f32)
            ).astype(bf16)
            second_copy(h, q).start()

    def send_third(q):
        all_of(first.at[:, 1, q], sends["first"], first_recv.at[1, q]).wait_recv()
        all_of(second.at[:, q], sends["second"], second_recv.at[q]).wait_recv()
        for h in range(2):
            third_src[h, q] = (
                partial[h, 3, q].astype(f32) + first[h, 1, q].astype(f32)
                + second[h, q].astype(f32)
            ).astype(bf16)
            if q != own:
                third_copy(h, q).start()
        if q == own:
            third_copy_own.start()

    third_copy_own = remote(
        third_src.at[other, own], third.at[own, me_s], sends["third"], third_recv.at[own],
        (me_t, me_c, other),
    )

    mask_rows(0)
    mark(0)
    grid_block(0, 0)
    send_first(0, 0)
    send_first(0, 1)
    relay(1)
    mark(1)
    grid_block(1, 0)
    send_first(1, 0)
    relay(2)
    mark(2)
    grid_block(2, 0)
    mark(3)
    mask_rows(1)
    grid_block(3, 0)
    send_second(0)
    send_first(1, 1)
    relay(3)
    loads[4].wait()
    pos = position[...]
    inner = pos % block
    code = (tile_ref[...] * n_chan + (pos // block) % n_chan) * 4
    code = code + (pos // (block * n_chan)) * 2 + inner // 128
    code_ids = lax.broadcasted_iota(jnp.int32, (n_tile * n_chan * 4, rows), 0)
    lane_ids = lax.broadcasted_iota(jnp.int32, (128, rows), 0)
    counts = lax.dot_general(
        (code_ids == code).astype(bf16), (lane_ids == inner % 128).astype(bf16),
        (((1,), (1,)), ((), ())), preferred_element_type=f32,
    )
    count_src[...] = counts.reshape(n_tile * n_chan * n_core, 2, 128)
    relay(4)
    for offset in offsets:
        count_copy(*offset).start()
    grid_block(0, 1)
    send_second(1)
    send_first(0, 2)
    grid_block(1, 1)
    send_first(1, 2)
    send_third(0)
    grid_block(2, 1)
    grid_block(3, 1)
    send_third(1)
    send_second(2)
    send_first(0, 3)
    send_first(1, 3)
    all_of(weights.at[0, :, 0:n_chan - 1], sends["weight"], recvs["weight"]).wait_recv()
    for o in range(1, n_chan):
        pass_copy(o).start()
    send_third(2)
    send_second(3)

    here = (me_t * n_core + me_s) * n_chan + me_c
    count = n_tile * n_core * n_chan
    hidden_all[0] = jnp.zeros((half_cols, 128), bf16)
    hidden_all[count + 1] = jnp.zeros((half_cols, 128), bf16)
    loads[5].wait()
    loads[6].wait()
    taps9 = depth_ref[...].astype(f32)
    taps9 = jnp.concatenate([taps9, taps9], axis=1)

    send_third(own)

    all_of(count_in.at[0:len(offsets)], sends["count"], recvs["count"]).wait_recv()
    mine = count_src[here_index(me_t, me_c, me_s, n_chan, n_core)]
    theirs = jnp.zeros(mine.shape, f32)
    for i in range(n_tile * n_chan):
        if i:
            mine = mine + count_in[i]
        theirs = theirs + count_in[n_tile * n_chan + i]

    for q in range(own):
        all_of(third.at[q], sends["third"], third_recv.at[q]).wait_recv()
    third_copy_own.wait_recv()
    for slot, counted in ((me_s, mine), (other, theirs)):
        summed = third[0, slot].astype(f32)
        for q in range(1, own):
            summed = summed + third[q, slot].astype(f32)
        if slot is me_s:
            summed = summed + third_src[me_s, own].astype(f32)
        else:
            summed = summed + third[own, slot].astype(f32)
        divisor = jnp.maximum(counted, 1.0)
        for u in range(block // 128):
            each = jnp.transpose(jnp.broadcast_to(divisor[u:u + 1, :], (128, 128)))
            means[slot, u * 128:(u + 1) * 128] = (summed[u * 128:(u + 1) * 128] / each).astype(bf16)

    all_of(weights.at[0, :, 0:n_chan - 1], sends["pass"], recvs["pass"]).wait_recv()
    lanes = weights.shape[3]
    encoded = jnp.zeros((quarter, n_chan * lanes), f32)
    for a in range(2):
        for b in range(2):
            at_row = (2 * a + b) * quarter
            fields = jnp.concatenate(
                [means[s, at_row:at_row + quarter] for s in range(n_core)], axis=1
            )
            encoded = encoded + lax.dot_general(
                fields, weights[a, b].reshape(n_chan * lanes, n_core * width),
                (((1,), (1,)), ((), ())), preferred_element_type=f32,
            )
    hidden = jax.nn.gelu(encoded)
    lane = lax.broadcasted_iota(jnp.int32, (half_cols, 128), 1)
    for g in range(n_chan // 2):
        upper = hidden[:half_cols, g * 128:(g + 1) * 128]
        lower = hidden[half_cols:, g * 128:(g + 1) * 128]
        hidden_src[2 * g] = jnp.where(lane < 64, upper, pltpu.roll(lower, 64, 1)).astype(bf16)
        hidden_src[2 * g + 1] = jnp.where(lane < 64, pltpu.roll(upper, 64, 1), lower).astype(bf16)

    def hidden_copy(i):
        to = at(*offsets[i])
        return remote(
            hidden_src.at[to[1]], hidden_all.at[here + 1], sends["hidden"], recvs["hidden"], to
        )

    on_edge = me_c % (n_chan - 1) == 0
    for i, (_, b, c) in enumerate(offsets):
        if c == 0:
            hidden_copy(i).start()

    @pl.when(on_edge)
    def _():
        for i, (_, b, c) in enumerate(offsets):
            if c:
                hidden_copy(i).start()

    hidden_all[here + 1] = hidden_src[me_c]
    all_of(first, sends["first"], first_recv.at[0, 0]).wait_send()
    all_of(second, sends["second"], second_recv.at[0]).wait_send()
    all_of(third.at[0:own], sends["third"], third_recv.at[0]).wait_send()
    all_of(third.at[own, 0], sends["third"], third_recv.at[own]).wait_send()
    all_of(weights.at[0, :, 0:n_chan - 1], sends["weight"], recvs["weight"]).wait_send()
    all_of(weights.at[0, :, 0:n_chan - 1], sends["pass"], recvs["pass"]).wait_send()
    all_of(count_in.at[0:len(offsets)], sends["count"], recvs["count"]).wait_send()
    every = n_tile * n_chan
    all_of(
        hidden_all.at[0:every - 1 + 2 * n_tile], sends["hidden"], recvs["hidden"]
    ).wait_recv()
    line = lax.broadcasted_iota(jnp.int32, (half_cols, 128), 0)
    for t in range(n_tile):
        j = jnp.int32(0)
        for i in range(n_chan):
            j = jnp.where(owners_ref[t, i] == me_t, i, j)
        at_piece = (t * n_core + me_s) * n_chan + j + 1
        total = jnp.zeros((half_cols, 128), f32)
        for p in range(3):
            field = hidden_all[at_piece + p - 1].astype(f32)
            before = jnp.where(line >= 2, pltpu.roll(field, 2, 0), 0.0)
            after = jnp.where(line < half_cols - 2, pltpu.roll(field, half_cols - 2, 0), 0.0)
            for q, shifted in enumerate((before, field, after)):
                total = total + shifted * taps9[3 * p + q:3 * p + q + 1, :]
            if p == 1:
                middle = field
        latent = middle + total
        out_ref[t, 0:half_cols] = latent[:, :64].astype(bf16)
        out_ref[t, half_cols:] = latent[:, 64:].astype(bf16)
    all_of(hidden_all.at[0:every - 1], sends["hidden"], recvs["hidden"]).wait_send()

    @pl.when(on_edge)
    def _():
        all_of(hidden_all.at[0:every], sends["hidden"], recvs["hidden"]).wait_send()


def here_index(t, c, s, n_chan, n_core):
    return (t * n_chan + c) * n_core + s


SENDS = ("first", "second", "third", "weight", "pass", "count", "hidden")
RECVS = ("weight", "pass", "count", "hidden")
RELAYS = 4


def fused(observed_values, observed_tile, observed_cell, patch_weight, depth_weight, owners):
    f32, bf16, i32 = jnp.float32, jnp.bfloat16, jnp.int32
    n_tile, n_chan, n_core = (lax.axis_size(a) for a in ("tile", "chan", "tm"))
    values = observed_values[0]
    rows, width = values.shape
    depth_in, lanes = patch_weight.shape[1:]
    turned = jnp.swapaxes(patch_weight, 1, 2).reshape(2, 2, lanes, depth_in)
    block = HS * WS // (n_core * n_chan)
    cells = block // 4
    dma, vmem = pltpu.SemaphoreType.DMA, pltpu.VMEM
    pieces = n_tile * n_core * n_chan
    out = pl.pallas_call(
        fused_kernel,
        out_shape=vmem((n_tile, cells, lanes), bf16),
        in_specs=[pl.BlockSpec(memory_space=pl.ANY)] * 7,
        out_specs=pl.BlockSpec(memory_space=pltpu.VMEM),
        scratch_shapes=[
            vmem((rows, width), bf16),
            vmem((rows // 128, 128), i32),
            vmem((1, rows), i32),
            vmem((1, rows), i32),
            vmem(depth_weight.shape, bf16),
            pltpu.SMEM(owners.shape, i32),
            *[vmem((rows, 2 * width), bf16)] * 2,
            *[vmem((2 * block, rows), bf16)] * 4,
            vmem((1, rows), i32),
            vmem((2, 4, n_tile, block, width), bf16),
            vmem((2, 2, n_tile, block, width), bf16),
            vmem((2, n_tile, block, width), bf16),
            vmem((2, n_tile, block, width), bf16),
            vmem((2, n_tile, block, width), bf16),
            vmem((n_tile, 2, block, width), bf16),
            vmem((pieces, 2, 128), f32),
            vmem((pieces, 2, 128), f32),
            vmem((2, 2, n_chan, lanes, depth_in), bf16),
            vmem((2, block, width), bf16),
            vmem((n_chan, cells // 2, 128), bf16),
            vmem((pieces + 2, cells // 2, 128), bf16),
            dma((7,)), dma((len(SENDS),)), dma((len(RECVS),)),
            dma((2, n_tile)), dma((n_tile,)), dma((n_tile,)),
            pltpu.SemaphoreType.REGULAR((RELAYS,)),
        ],
        compiler_params=pltpu.CompilerParams(
            collective_id=0, has_side_effects=True, vmem_limit_bytes=56 * 2**20
        ),
    )(
        values, observed_tile.reshape(rows // 128, 128), observed_tile.reshape(1, rows),
        observed_cell, turned, depth_weight, owners,
    )
    return out.reshape(1, 1, n_tile, cells, lanes)


def fits(mesh):
    tile, chan, tm = (mesh.shape[a] for a in ("tile", "chan", "tm"))
    return tile == 4 and chan == 4 and tm == 2


def solution(mesh):
    placed = (
        P("tm", ("tile", "chan"), None),
        P("tm", ("tile", "chan"), None),
        P("tm", ("tile", "chan")),
        P(None, None, "chan"),
        P(None, "chan"),
        P(),
    )
    return jax.shard_map(
        fused if fits(mesh) else local,
        mesh=mesh,
        in_specs=placed,
        out_specs=P("tile", "tm", None, None, "chan"),
        check_vma=False,
    )
```

```python
import functools
import jax
import jax.numpy as jnp
from jax import lax
from jax.experimental import pallas as pl
from jax.experimental.pallas import tpu as pltpu
from jax.sharding import PartitionSpec as P

V = 128
HS = 32
WS = 64


def padded(x, sides, width):
    for axis, dim in sides:
        devices, length = (lax.axis_size(axis), x.shape[dim])
        up = [(i, (i + 1) % devices) for i in range(devices - 1)]
        down = [(j, i) for i, j in up]
        last = lax.slice_in_dim(x, length - width, length, axis=dim)
        first = lax.slice_in_dim(x, 0, width, axis=dim)
        before = lax.ppermute(last, axis, up)
        after = lax.ppermute(first, axis, down)
        x = jnp.concatenate([before, x, after], axis=dim)
    return x


def pack_rows(values, destination, placed, tile_count, capacity):
    match = (destination[:, None] == lax.iota(jnp.int32, tile_count)[None, :]).astype(jnp.int32)
    earlier = jnp.cumsum(match, axis=0) - match
    position = jnp.sum(earlier * match, axis=1)
    slot_index = destination * capacity + position
    width = values.shape[1]
    sent_values = jnp.zeros((tile_count * capacity, width), jnp.bfloat16).at[slot_index].set(values)
    sent_cells = jnp.full((tile_count * capacity,), -1, jnp.int32).at[slot_index].set(placed)
    return (
        sent_values.reshape(tile_count, capacity, width),
        sent_cells.reshape(tile_count, capacity),
    )


def grid_block(arrived_values, arrived_cells, first_cell):
    cell_ids = first_cell + lax.iota(jnp.int32, 128)
    matches = cell_ids[:, None] == arrived_cells[None, :]
    totals = jnp.dot(
        matches.astype(jnp.bfloat16), arrived_values, preferred_element_type=jnp.float32
    )
    counts = jnp.sum(matches.astype(jnp.float32), axis=1)
    return (totals, counts)


def patch_rows(field, weight, row_start, row_count):
    slab = lax.dynamic_slice_in_dim(field, 2 * row_start, 2 * row_count, 0)
    depth_in = field.shape[2]
    result = jnp.zeros((row_count * (field.shape[1] // 2), weight.shape[2]), jnp.float32)
    for tap_row in range(2):
        for tap_col in range(2):
            window = slab[tap_row::2, tap_col::2, :].reshape(-1, depth_in)
            result = result + jnp.dot(
                window, weight[tap_row * 2 + tap_col], preferred_element_type=jnp.float32
            )
    return result.reshape(row_count, field.shape[1] // 2, weight.shape[2])


def local(observed_values, observed_tile, observed_cell, patch_weight, depth_weight, owners):
    tile_count = lax.axis_size("tile")
    slot_count = lax.axis_size("tm")
    values = observed_values[0]
    capacity = 2 * values.shape[0] // tile_count
    sent_values, sent_cells = pack_rows(
        values, observed_tile[0, :, 0], observed_cell[0], tile_count, capacity
    )
    arrived = (
        lax.all_to_all(sent_values, "tile", split_axis=0, concat_axis=0, tiled=True),
        lax.all_to_all(sent_cells, "tile", split_axis=0, concat_axis=0, tiled=True),
    )
    arrived_values = arrived[0].reshape(-1, V)
    arrived_cells = arrived[1].reshape(-1)
    cell_count = HS * WS
    firsts = jnp.arange(cell_count // 128, dtype=jnp.int32) * 128
    totals, counts = lax.map(
        lambda first_cell: grid_block(arrived_values, arrived_cells, first_cell), firsts
    )
    totals = totals.reshape(cell_count, V)
    counts = counts.reshape(cell_count)
    totals, counts = (
        lax.psum(totals.astype(jnp.bfloat16), "chan").astype(jnp.float32),
        lax.psum(counts.astype(jnp.bfloat16), "chan").astype(jnp.float32),
    )
    means = (totals / jnp.maximum(counts, 1.0)[:, None]).astype(jnp.bfloat16)
    means = means.reshape(HS, WS, V)
    out_rows = HS // (2 * slot_count)
    half_cols = WS // 2
    stacked = lax.all_gather(means, "tm", axis=2, tiled=True)
    encoded = patch_rows(stacked, patch_weight, lax.axis_index("tm") * out_rows, out_rows)
    hidden = jax.nn.gelu(encoded).astype(jnp.bfloat16)
    rimmed = padded(hidden, ((("tile", "tm"), 0),), 2)
    widened = jnp.pad(rimmed, ((0, 0), (2, 2), (0, 0))).astype(jnp.float32)
    depth = jnp.zeros(hidden.shape, jnp.float32)
    for tap_row in range(3):
        for tap_col in range(3):
            shifted = widened[
                2 * tap_row : 2 * tap_row + out_rows, 2 * tap_col : 2 * tap_col + half_cols, :
            ]
            depth = depth + shifted * depth_weight[tap_row * 3 + tap_col].astype(jnp.float32)
    latent = (hidden.astype(jnp.float32) + depth).astype(jnp.bfloat16)
    channels = latent.shape[2]
    pieces = latent.reshape(tile_count, -1, channels)
    own_row = lax.dynamic_index_in_dim(owners, lax.axis_index("tile"), 0, keepdims=False)
    order = lax.iota(jnp.int32, tile_count)
    chosen = jnp.sum(
        order[None, :] * (own_row[None, :] == order[:, None]).astype(jnp.int32), axis=1
    )
    outgoing = pieces[chosen]
    received = lax.all_to_all(outgoing, "tile", split_axis=0, concat_axis=0, tiled=True)
    return received.reshape(1, 1, tile_count, -1, channels)


def fused_kernel(
    values_hbm, column_hbm, tile_hbm, cell_hbm, weight_hbm, depth_hbm, owners_hbm, out_ref,
    values_ref, column_ref, tile_ref, cell_ref, depth_ref, owners_ref,
    masked_a, masked_b, onehot_a, onehot_b, onehot_c, onehot_d, position, partial, first, second_src, second, third_src, third, early,
    count_src, count_in, weights, means, hidden_src, hidden_all,
    load_sems, send_sems, recv_sems, first_recv, second_recv, third_recv,
    early_recv, relays,
):
    f32, bf16 = jnp.float32, jnp.bfloat16
    n_tile, n_chan, n_core = (lax.axis_size(a) for a in ("tile", "chan", "tm"))
    me_t, me_c, me_s = (lax.axis_index(a) for a in ("tile", "chan", "tm"))
    rows, width = values_ref.shape
    block = partial.shape[3]
    quarter = block // 4
    half_cols = WS // 2
    flip_x = me_c + 1 - 2 * (me_c % 2)
    flip_y = (me_c + 2) % 4
    diagonal = 3 - me_c
    near = (flip_x, flip_y)
    far = (flip_y, flip_x)
    other = 1 - me_s
    masked = (masked_a, masked_b)
    onehot = (onehot_a, onehot_b, onehot_c, onehot_d)
    shifts = (2, 3, 1, 0)
    half = block // 2
    split = 1
    own = n_tile - 1
    sends = {n: send_sems.at[i] for i, n in enumerate(SENDS)}
    recvs = {n: recv_sems.at[i] for i, n in enumerate(RECVS)}

    def remote(source, target, send, recv, device):
        return pltpu.make_async_remote_copy(
            src_ref=source, dst_ref=target, send_sem=send, recv_sem=recv,
            device_id=device, device_id_type=pl.DeviceIdType.MESH,
        )

    def signal(sem, device):
        pl.semaphore_signal(sem, inc=1, device_id=device, device_id_type=pl.DeviceIdType.MESH)

    def all_of(ref, send, recv):
        return remote(ref, ref, send, recv, (me_t, me_c, other))

    offsets = [
        (a, b, c) for a in range(n_tile) for b in range(n_chan) for c in range(n_core)
    ][1:]
    offsets = sorted(offsets, key=lambda o: (2, 1, 3, 0).index(o[0]))

    def at(a, b, c):
        return ((me_t + a) % n_tile, (me_c + b) % n_chan, (me_s + c) % n_core)

    loads = [
        pltpu.make_async_copy(source, target, load_sems.at[i])
        for i, (source, target) in enumerate((
            (weight_hbm, weights.at[:, :, me_c]), (column_hbm, column_ref), (cell_hbm, cell_ref),
            (values_hbm, values_ref), (tile_hbm, tile_ref), (depth_hbm, depth_ref),
            (owners_hbm, owners_ref),
        ))
    ]
    for i in (2, 1, 3, 0, 4, 5, 6):
        loads[i].start()

    def signal_near(sem):
        for o in range(1, n_chan):
            signal(sem, (me_t, (me_c + o) % n_chan, me_s))
        signal(sem, (me_t, me_c, other))

        @pl.when(me_t > 0)
        def _():
            signal(sem, (me_t - 1, me_c, me_s))

        @pl.when(me_t < n_tile - 1)
        def _():
            signal(sem, (me_t + 1, me_c, me_s))

    def wait_near(sem):
        inner_tile = jnp.where((me_t > 0) & (me_t < n_tile - 1), 1, 0)
        pl.semaphore_wait(sem, n_chan + 1 + inner_tile)

    def relay(i):
        if i:
            wait_near(relays.at[i - 1])
        if i < RELAYS:
            signal_near(relays.at[i])

    barrier = pltpu.get_barrier_semaphore()
    signal_near(barrier)

    def weight_copy(to):
        here = weights.at[me_s, :, me_c]
        recv = recvs["cross" if to is diagonal else "weight"]
        return remote(here, here, sends["weight"], recv, (me_t, to, me_s))

    def pass_copy(of):
        here = weights.at[me_s, :, of]
        return remote(here, here, sends["pass"], recvs["pass"], (me_t, me_c, other))

    def count_copy(a, b, c):
        to = at(a, b, c)
        return remote(
            count_src.at[(to[0] * n_chan + to[1]) * n_core + to[2]],
            count_in.at[(c * n_tile + a) * n_chan + b],
            sends["count"], recvs["count"], to,
        )

    def kept(q):
        return pl.ds(half, half) if q == split else pl.ds(0, block)

    def first_copy(h, k, q):
        return remote(
            partial.at[h, k, q, kept(q)], first.at[h, k, q, kept(q)],
            sends["first"], first_recv.at[k, q], (me_t, near[h], me_s),
        )

    def second_copy(h, q):
        return remote(
            second_src.at[h, q, kept(q)], second.at[h, q, kept(q)],
            sends["second"], second_recv.at[q], (me_t, far[h], me_s),
        )

    def third_copy(h, q):
        return remote(
            third_src.at[h, q, kept(q)], third.at[q, me_s, kept(q)],
            sends["third"], third_recv.at[q], ((me_t + shifts[q]) % n_tile, me_c, h),
        )

    def early_copy(h, k):
        return remote(
            partial.at[h, k, split, pl.ds(0, half)], early.at[h, k],
            sends["early"], early_recv.at[k], ((me_t + shifts[split]) % n_tile, me_c, me_s),
        )

    def send_early(k):
        for h in range(2):
            early_copy(h, k).start()

    def wait_early(k):
        all_of(early.at[:, k], sends["early"], early_recv.at[k]).wait_recv()

    loads[2].wait()
    cell = cell_ref[...]
    row, col = cell // WS, cell % WS
    position[...] = (
        (row // 4) * block + (row % 2) * (2 * quarter) + (col % 2) * quarter
        + ((row % 4) // 2) * half_cols + col // 2
    )
    loads[0].wait()
    wait_near(barrier)
    weight_copy(flip_x).start()
    weight_copy(flip_y).start()
    relay(0)
    loads[1].wait()
    columns = jnp.transpose(column_ref[...].astype(f32))
    loads[3].wait()

    def mask_rows(pair):
        for i in range(rows // 128):
            tiles = jnp.broadcast_to(columns[:, i:i + 1], (128, width)).astype(bf16)
            taken = values_ref[i * 128:(i + 1) * 128, :]
            for u in range(2):
                wanted = ((me_t + shifts[2 * pair + u]) % n_tile).astype(f32).astype(bf16)
                masked[pair][i * 128:(i + 1) * 128, u * width:(u + 1) * width] = jnp.where(
                    tiles == wanted, taken, jnp.zeros_like(taken)
                )

    ids = lax.broadcasted_iota(jnp.int32, (block, rows), 0).astype(bf16)

    def mark(k):
        for h in range(2):
            j = (diagonal, near[h], far[h], me_c)[k]
            offset = (position[...] - (h * n_chan + j) * block).astype(bf16)
            onehot[k][h * block:(h + 1) * block] = jnp.where(
                ids == offset, jnp.ones((), bf16), jnp.zeros((), bf16)
            )

    def grid_block(k, pair):
        sums = [
            jnp.dot(
                onehot[k][h * block:(h + 1) * block], masked[pair][...],
                preferred_element_type=f32,
            )
            for h in range(2)
        ]
        for h in range(2):
            for u in range(2):
                partial[h, k, 2 * pair + u] = sums[h][:, u * width:(u + 1) * width].astype(bf16)

    def send_first(k, q):
        if q == own:
            wait_early(k)
        for h in range(2):
            if q == own:
                partial[h, k, q, 0:half] = (
                    partial[h, k, q, 0:half].astype(f32) + early[h, k].astype(f32)
                ).astype(bf16)
            first_copy(h, k, q).start()

    def combined(h, k, q, arrived):
        total = partial[h, k, q, kept(q)].astype(f32)
        for ref in arrived:
            total = total + ref[kept(q)].astype(f32)
        if q == own:
            total = jnp.concatenate(
                [total[:half] + early[h, k].astype(f32), total[half:]], axis=0
            )
        return total.astype(bf16)

    def send_second(q):
        all_of(first.at[:, 0, q, kept(q)], sends["first"], first_recv.at[0, q]).wait_recv()
        if q == own:
            wait_early(2)
        for h in range(2):
            second_src[h, q, kept(q)] = combined(h, 2, q, (first.at[h, 0, q],))
            second_copy(h, q).start()

    def send_third(q):
        all_of(first.at[:, 1, q, kept(q)], sends["first"], first_recv.at[1, q]).wait_recv()
        all_of(second.at[:, q, kept(q)], sends["second"], second_recv.at[q]).wait_recv()
        if q == own:
            wait_early(3)
        for h in range(2):
            third_src[h, q, kept(q)] = combined(h, 3, q, (first.at[h, 1, q], second.at[h, q]))
            if q != own:
                third_copy(h, q).start()
        if q == own:
            third_copy_own.start()

    third_copy_own = remote(
        third_src.at[other, own], third.at[own, me_s], sends["third"], third_recv.at[own],
        (me_t, me_c, other),
    )

    mask_rows(0)
    mark(0)
    grid_block(0, 0)
    send_first(0, 0)
    send_first(0, 1)
    relay(1)
    mark(1)
    grid_block(1, 0)
    send_first(1, 0)
    send_first(1, 1)
    relay(2)
    send_early(0)
    send_early(1)
    mark(2)
    grid_block(2, 0)
    send_early(2)
    send_second(0)
    mark(3)
    mask_rows(1)
    grid_block(3, 0)
    send_early(3)
    send_second(1)
    relay(3)
    grid_block(0, 1)
    send_first(0, 2)
    loads[4].wait()
    pos = position[...]
    inner = pos % block
    code = (tile_ref[...] * n_chan + (pos // block) % n_chan) * 4
    code = code + (pos // (block * n_chan)) * 2 + inner // 128
    code_ids = lax.broadcasted_iota(jnp.int32, (n_tile * n_chan * 4, rows), 0)
    lane_ids = lax.broadcasted_iota(jnp.int32, (128, rows), 0)
    counts = lax.dot_general(
        (code_ids == code).astype(bf16), (lane_ids == inner % 128).astype(bf16),
        (((1,), (1,)), ((), ())), preferred_element_type=f32,
    )
    count_src[...] = counts.reshape(n_tile * n_chan * n_core, 2, 128)
    relay(4)
    for offset in offsets:
        count_copy(*offset).start()
    grid_block(1, 1)
    send_first(1, 2)
    send_third(0)
    send_third(1)
    grid_block(2, 1)
    send_second(2)
    send_first(0, 3)
    send_first(1, 3)
    weight_copy(diagonal).start()
    grid_block(3, 1)
    all_of(weights.at[0, :, 0:2], sends["weight"], recvs["weight"]).wait_recv()
    pass_copy(flip_x).start()
    pass_copy(flip_y).start()
    send_third(2)
    send_second(3)

    here = (me_t * n_core + me_s) * n_chan + me_c
    count = n_tile * n_core * n_chan
    hidden_all[0] = jnp.zeros((half_cols, 128), bf16)
    hidden_all[count + 1] = jnp.zeros((half_cols, 128), bf16)
    loads[5].wait()
    loads[6].wait()
    taps9 = depth_ref[...].astype(f32)
    taps9 = jnp.concatenate([taps9, taps9], axis=1)

    all_of(weights.at[0, :, 0], sends["weight"], recvs["cross"]).wait_recv()
    pass_copy(diagonal).start()
    send_third(own)

    all_of(count_in.at[0:len(offsets)], sends["count"], recvs["count"]).wait_recv()
    mine = count_src[here_index(me_t, me_c, me_s, n_chan, n_core)]
    theirs = jnp.zeros(mine.shape, f32)
    for i in range(n_tile * n_chan):
        if i:
            mine = mine + count_in[i]
        theirs = theirs + count_in[n_tile * n_chan + i]

    for q in range(own):
        all_of(third.at[q, :, kept(q)], sends["third"], third_recv.at[q]).wait_recv()
    third_copy_own.wait_recv()
    for slot, counted in ((me_s, mine), (other, theirs)):
        summed = third[0, slot].astype(f32) + third[2, slot].astype(f32)
        summed = jnp.concatenate(
            [summed[:half], summed[half:] + third[split, slot, half:].astype(f32)], axis=0
        )
        if slot is me_s:
            summed = summed + third_src[me_s, own].astype(f32)
        else:
            summed = summed + third[own, slot].astype(f32)
        divisor = jnp.maximum(counted, 1.0)
        for u in range(block // 128):
            each = jnp.transpose(jnp.broadcast_to(divisor[u:u + 1, :], (128, 128)))
            means[slot, u * 128:(u + 1) * 128] = (summed[u * 128:(u + 1) * 128] / each).astype(bf16)

    all_of(weights.at[0, :, 0:n_chan - 1], sends["pass"], recvs["pass"]).wait_recv()
    lanes = weights.shape[3]
    encoded = jnp.zeros((quarter, n_chan * lanes), f32)
    for a in range(2):
        for b in range(2):
            at_row = (2 * a + b) * quarter
            fields = jnp.concatenate(
                [means[s, at_row:at_row + quarter] for s in range(n_core)], axis=1
            )
            encoded = encoded + lax.dot_general(
                fields, weights[a, b].reshape(n_chan * lanes, n_core * width),
                (((1,), (1,)), ((), ())), preferred_element_type=f32,
            )
    hidden = jax.nn.gelu(encoded)
    lane = lax.broadcasted_iota(jnp.int32, (half_cols, 128), 1)
    for g in range(n_chan // 2):
        upper = hidden[:half_cols, g * 128:(g + 1) * 128]
        lower = hidden[half_cols:, g * 128:(g + 1) * 128]
        hidden_src[2 * g] = jnp.where(lane < 64, upper, pltpu.roll(lower, 64, 1)).astype(bf16)
        hidden_src[2 * g + 1] = jnp.where(lane < 64, pltpu.roll(upper, 64, 1), lower).astype(bf16)

    def hidden_copy(i):
        to = at(*offsets[i])
        return remote(
            hidden_src.at[to[1]], hidden_all.at[here + 1], sends["hidden"], recvs["hidden"], to
        )

    on_edge = me_c % (n_chan - 1) == 0
    for i, (_, b, c) in enumerate(offsets):
        if c == 0:
            hidden_copy(i).start()

    @pl.when(on_edge)
    def _():
        for i, (_, b, c) in enumerate(offsets):
            if c:
                hidden_copy(i).start()

    hidden_all[here + 1] = hidden_src[me_c]
    most = pl.ds(0, block - half // n_tile)
    all_of(first.at[:, :, :, most], sends["first"], first_recv.at[0, 0]).wait_send()
    all_of(second.at[:, :, most], sends["second"], second_recv.at[0]).wait_send()
    all_of(third.at[0:own], sends["third"], third_recv.at[0]).wait_send()
    all_of(early, sends["early"], early_recv.at[0]).wait_send()
    all_of(weights.at[0, :, 0:n_chan - 1], sends["weight"], recvs["weight"]).wait_send()
    all_of(weights.at[0, :, 0:n_chan - 1], sends["pass"], recvs["pass"]).wait_send()
    all_of(count_in.at[0:len(offsets)], sends["count"], recvs["count"]).wait_send()
    every = n_tile * n_chan
    all_of(
        hidden_all.at[0:every - 1 + 2 * n_tile], sends["hidden"], recvs["hidden"]
    ).wait_recv()
    line = lax.broadcasted_iota(jnp.int32, (half_cols, 128), 0)
    for t in range(n_tile):
        j = jnp.int32(0)
        for i in range(n_chan):
            j = jnp.where(owners_ref[t, i] == me_t, i, j)
        at_piece = (t * n_core + me_s) * n_chan + j + 1
        total = jnp.zeros((half_cols, 128), f32)
        for p in range(3):
            field = hidden_all[at_piece + p - 1].astype(f32)
            before = jnp.where(line >= 2, pltpu.roll(field, 2, 0), 0.0)
            after = jnp.where(line < half_cols - 2, pltpu.roll(field, half_cols - 2, 0), 0.0)
            for q, shifted in enumerate((before, field, after)):
                total = total + shifted * taps9[3 * p + q:3 * p + q + 1, :]
            if p == 1:
                middle = field
        latent = middle + total
        out_ref[t, 0:half_cols] = latent[:, :64].astype(bf16)
        out_ref[t, half_cols:] = latent[:, 64:].astype(bf16)
    all_of(hidden_all.at[0:every - 1], sends["hidden"], recvs["hidden"]).wait_send()

    @pl.when(on_edge)
    def _():
        all_of(hidden_all.at[0:every], sends["hidden"], recvs["hidden"]).wait_send()


def here_index(t, c, s, n_chan, n_core):
    return (t * n_chan + c) * n_core + s


SENDS = ("first", "second", "third", "weight", "pass", "count", "hidden", "early")
RECVS = ("weight", "cross", "pass", "count", "hidden")
RELAYS = 4


def fused(observed_values, observed_tile, observed_cell, patch_weight, depth_weight, owners):
    f32, bf16, i32 = jnp.float32, jnp.bfloat16, jnp.int32
    n_tile, n_chan, n_core = (lax.axis_size(a) for a in ("tile", "chan", "tm"))
    values = observed_values[0]
    rows, width = values.shape
    depth_in, lanes = patch_weight.shape[1:]
    turned = jnp.swapaxes(patch_weight, 1, 2).reshape(2, 2, lanes, depth_in)
    block = HS * WS // (n_core * n_chan)
    cells = block // 4
    dma, vmem = pltpu.SemaphoreType.DMA, pltpu.VMEM
    pieces = n_tile * n_core * n_chan
    out = pl.pallas_call(
        fused_kernel,
        out_shape=vmem((n_tile, cells, lanes), bf16),
        in_specs=[pl.BlockSpec(memory_space=pl.ANY)] * 7,
        out_specs=pl.BlockSpec(memory_space=pltpu.VMEM),
        scratch_shapes=[
            vmem((rows, width), bf16),
            vmem((rows // 128, 128), i32),
            vmem((1, rows), i32),
            vmem((1, rows), i32),
            vmem(depth_weight.shape, bf16),
            pltpu.SMEM(owners.shape, i32),
            *[vmem((rows, 2 * width), bf16)] * 2,
            *[vmem((2 * block, rows), bf16)] * 4,
            vmem((1, rows), i32),
            vmem((2, 4, n_tile, block, width), bf16),
            vmem((2, 2, n_tile, block, width), bf16),
            vmem((2, n_tile, block, width), bf16),
            vmem((2, n_tile, block, width), bf16),
            vmem((2, n_tile, block, width), bf16),
            vmem((n_tile, 2, block, width), bf16),
            vmem((2, 4, block // 2, width), bf16),
            vmem((pieces, 2, 128), f32),
            vmem((pieces, 2, 128), f32),
            vmem((2, 2, n_chan, lanes, depth_in), bf16),
            vmem((2, block, width), bf16),
            vmem((n_chan, cells // 2, 128), bf16),
            vmem((pieces + 2, cells // 2, 128), bf16),
            dma((7,)), dma((len(SENDS),)), dma((len(RECVS),)),
            dma((2, n_tile)), dma((n_tile,)), dma((n_tile,)), dma((4,)),
            pltpu.SemaphoreType.REGULAR((RELAYS,)),
        ],
        compiler_params=pltpu.CompilerParams(
            collective_id=0, has_side_effects=True, vmem_limit_bytes=56 * 2**20
        ),
    )(
        values, observed_tile.reshape(rows // 128, 128), observed_tile.reshape(1, rows),
        observed_cell, turned, depth_weight, owners,
    )
    return out.reshape(1, 1, n_tile, cells, lanes)


def fits(mesh):
    tile, chan, tm = (mesh.shape[a] for a in ("tile", "chan", "tm"))
    return tile == 4 and chan == 4 and tm == 2


def solution(mesh):
    placed = (
        P("tm", ("tile", "chan"), None),
        P("tm", ("tile", "chan"), None),
        P("tm", ("tile", "chan")),
        P(None, None, "chan"),
        P(None, "chan"),
        P(),
    )
    return jax.shard_map(
        fused if fits(mesh) else local,
        mesh=mesh,
        in_specs=placed,
        out_specs=P("tile", "tm", None, None, "chan"),
        check_vma=False,
    )
```

```python
import functools
import jax
import jax.numpy as jnp
from jax import lax
from jax.experimental import pallas as pl
from jax.experimental.pallas import tpu as pltpu
from jax.sharding import PartitionSpec as P

V = 128
HS = 32
WS = 64


def padded(x, sides, width):
    for axis, dim in sides:
        devices, length = (lax.axis_size(axis), x.shape[dim])
        up = [(i, (i + 1) % devices) for i in range(devices - 1)]
        down = [(j, i) for i, j in up]
        last = lax.slice_in_dim(x, length - width, length, axis=dim)
        first = lax.slice_in_dim(x, 0, width, axis=dim)
        before = lax.ppermute(last, axis, up)
        after = lax.ppermute(first, axis, down)
        x = jnp.concatenate([before, x, after], axis=dim)
    return x


def pack_rows(values, destination, placed, tile_count, capacity):
    match = (destination[:, None] == lax.iota(jnp.int32, tile_count)[None, :]).astype(jnp.int32)
    earlier = jnp.cumsum(match, axis=0) - match
    position = jnp.sum(earlier * match, axis=1)
    slot_index = destination * capacity + position
    width = values.shape[1]
    sent_values = jnp.zeros((tile_count * capacity, width), jnp.bfloat16).at[slot_index].set(values)
    sent_cells = jnp.full((tile_count * capacity,), -1, jnp.int32).at[slot_index].set(placed)
    return (
        sent_values.reshape(tile_count, capacity, width),
        sent_cells.reshape(tile_count, capacity),
    )


def grid_block(arrived_values, arrived_cells, first_cell):
    cell_ids = first_cell + lax.iota(jnp.int32, 128)
    matches = cell_ids[:, None] == arrived_cells[None, :]
    totals = jnp.dot(
        matches.astype(jnp.bfloat16), arrived_values, preferred_element_type=jnp.float32
    )
    counts = jnp.sum(matches.astype(jnp.float32), axis=1)
    return (totals, counts)


def patch_rows(field, weight, row_start, row_count):
    slab = lax.dynamic_slice_in_dim(field, 2 * row_start, 2 * row_count, 0)
    depth_in = field.shape[2]
    result = jnp.zeros((row_count * (field.shape[1] // 2), weight.shape[2]), jnp.float32)
    for tap_row in range(2):
        for tap_col in range(2):
            window = slab[tap_row::2, tap_col::2, :].reshape(-1, depth_in)
            result = result + jnp.dot(
                window, weight[tap_row * 2 + tap_col], preferred_element_type=jnp.float32
            )
    return result.reshape(row_count, field.shape[1] // 2, weight.shape[2])


def local(observed_values, observed_tile, observed_cell, patch_weight, depth_weight, owners):
    tile_count = lax.axis_size("tile")
    slot_count = lax.axis_size("tm")
    values = observed_values[0]
    capacity = 2 * values.shape[0] // tile_count
    sent_values, sent_cells = pack_rows(
        values, observed_tile[0, :, 0], observed_cell[0], tile_count, capacity
    )
    arrived = (
        lax.all_to_all(sent_values, "tile", split_axis=0, concat_axis=0, tiled=True),
        lax.all_to_all(sent_cells, "tile", split_axis=0, concat_axis=0, tiled=True),
    )
    arrived_values = arrived[0].reshape(-1, V)
    arrived_cells = arrived[1].reshape(-1)
    cell_count = HS * WS
    firsts = jnp.arange(cell_count // 128, dtype=jnp.int32) * 128
    totals, counts = lax.map(
        lambda first_cell: grid_block(arrived_values, arrived_cells, first_cell), firsts
    )
    totals = totals.reshape(cell_count, V)
    counts = counts.reshape(cell_count)
    totals, counts = (
        lax.psum(totals.astype(jnp.bfloat16), "chan").astype(jnp.float32),
        lax.psum(counts.astype(jnp.bfloat16), "chan").astype(jnp.float32),
    )
    means = (totals / jnp.maximum(counts, 1.0)[:, None]).astype(jnp.bfloat16)
    means = means.reshape(HS, WS, V)
    out_rows = HS // (2 * slot_count)
    half_cols = WS // 2
    stacked = lax.all_gather(means, "tm", axis=2, tiled=True)
    encoded = patch_rows(stacked, patch_weight, lax.axis_index("tm") * out_rows, out_rows)
    hidden = jax.nn.gelu(encoded).astype(jnp.bfloat16)
    rimmed = padded(hidden, ((("tile", "tm"), 0),), 2)
    widened = jnp.pad(rimmed, ((0, 0), (2, 2), (0, 0))).astype(jnp.float32)
    depth = jnp.zeros(hidden.shape, jnp.float32)
    for tap_row in range(3):
        for tap_col in range(3):
            shifted = widened[
                2 * tap_row : 2 * tap_row + out_rows, 2 * tap_col : 2 * tap_col + half_cols, :
            ]
            depth = depth + shifted * depth_weight[tap_row * 3 + tap_col].astype(jnp.float32)
    latent = (hidden.astype(jnp.float32) + depth).astype(jnp.bfloat16)
    channels = latent.shape[2]
    pieces = latent.reshape(tile_count, -1, channels)
    own_row = lax.dynamic_index_in_dim(owners, lax.axis_index("tile"), 0, keepdims=False)
    order = lax.iota(jnp.int32, tile_count)
    chosen = jnp.sum(
        order[None, :] * (own_row[None, :] == order[:, None]).astype(jnp.int32), axis=1
    )
    outgoing = pieces[chosen]
    received = lax.all_to_all(outgoing, "tile", split_axis=0, concat_axis=0, tiled=True)
    return received.reshape(1, 1, tile_count, -1, channels)


def fused_kernel(
    values_hbm, column_hbm, tile_hbm, cell_hbm, weight_hbm, depth_hbm, owners_hbm, out_ref,
    values_ref, column_ref, tile_ref, cell_ref, depth_ref, owners_ref,
    masked_a, masked_b, onehot_a, onehot_b, onehot_c, onehot_d, position, partial, first, second_src, second, third_src, third, early,
    count_src, count_in, weights, means, hidden_src, hidden_all,
    load_sems, send_sems, recv_sems, first_recv, second_recv, third_recv,
    early_recv, hidden_recv, relays,
):
    f32, bf16 = jnp.float32, jnp.bfloat16
    n_tile, n_chan, n_core = (lax.axis_size(a) for a in ("tile", "chan", "tm"))
    me_t, me_c, me_s = (lax.axis_index(a) for a in ("tile", "chan", "tm"))
    rows, width = values_ref.shape
    block = partial.shape[3]
    quarter = block // 4
    half_cols = WS // 2
    flip_x = me_c + 1 - 2 * (me_c % 2)
    flip_y = (me_c + 2) % 4
    diagonal = 3 - me_c
    near = (flip_x, flip_y)
    far = (flip_y, flip_x)
    other = 1 - me_s
    masked = (masked_a, masked_b)
    onehot = (onehot_a, onehot_b, onehot_c, onehot_d)
    shifts = (2, 3, 1, 0)
    half = block // 2
    split = 1
    own = n_tile - 1
    sends = {n: send_sems.at[i] for i, n in enumerate(SENDS)}
    recvs = {n: recv_sems.at[i] for i, n in enumerate(RECVS)}

    def remote(source, target, send, recv, device):
        return pltpu.make_async_remote_copy(
            src_ref=source, dst_ref=target, send_sem=send, recv_sem=recv,
            device_id=device, device_id_type=pl.DeviceIdType.MESH,
        )

    def signal(sem, device):
        pl.semaphore_signal(sem, inc=1, device_id=device, device_id_type=pl.DeviceIdType.MESH)

    def all_of(ref, send, recv):
        return remote(ref, ref, send, recv, (me_t, me_c, other))

    offsets = [
        (a, b, c) for a in range(n_tile) for b in range(n_chan) for c in range(n_core)
    ][1:]

    def at(a, b, c):
        return ((me_t + a) % n_tile, (me_c + b) % n_chan, (me_s + c) % n_core)

    loads = [
        pltpu.make_async_copy(source, target, load_sems.at[i])
        for i, (source, target) in enumerate((
            (weight_hbm, weights.at[:, :, me_c]), (column_hbm, column_ref), (cell_hbm, cell_ref),
            (values_hbm, values_ref), (tile_hbm, tile_ref), (depth_hbm, depth_ref),
            (owners_hbm, owners_ref),
        ))
    ]
    for i in (2, 1, 3, 0, 4, 5, 6):
        loads[i].start()

    def signal_near(sem):
        for o in range(1, n_chan):
            signal(sem, (me_t, (me_c + o) % n_chan, me_s))
        signal(sem, (me_t, me_c, other))

        @pl.when(me_t > 0)
        def _():
            signal(sem, (me_t - 1, me_c, me_s))

        @pl.when(me_t < n_tile - 1)
        def _():
            signal(sem, (me_t + 1, me_c, me_s))

    def wait_near(sem):
        inner_tile = jnp.where((me_t > 0) & (me_t < n_tile - 1), 1, 0)
        pl.semaphore_wait(sem, n_chan + 1 + inner_tile)

    def relay(i):
        if i:
            wait_near(relays.at[i - 1])
        if i < RELAYS:
            signal_near(relays.at[i])

    barrier = pltpu.get_barrier_semaphore()
    signal_near(barrier)

    def weight_copy(to):
        here = weights.at[me_s, :, me_c]
        recv = recvs["cross" if to is diagonal else "weight"]
        return remote(here, here, sends["weight"], recv, (me_t, to, me_s))

    def pass_copy(of):
        here = weights.at[me_s, :, of]
        return remote(here, here, sends["pass"], recvs["pass"], (me_t, me_c, other))

    def count_copy(a, b, c):
        to = at(a, b, c)
        return remote(
            count_src.at[(to[0] * n_chan + to[1]) * n_core + to[2]],
            count_in.at[(c * n_tile + a) * n_chan + b],
            sends["count"], recvs["count"], to,
        )

    def kept(q):
        return pl.ds(half, half) if q == split else pl.ds(0, block)

    def first_copy(h, k, q):
        return remote(
            partial.at[h, k, q, kept(q)], first.at[h, k, q, kept(q)],
            sends["first"], first_recv.at[k, q], (me_t, near[h], me_s),
        )

    def second_copy(h, q):
        return remote(
            second_src.at[h, q, kept(q)], second.at[h, q, kept(q)],
            sends["second"], second_recv.at[q], (me_t, far[h], me_s),
        )

    def third_copy(h, q):
        return remote(
            third_src.at[h, q, kept(q)], third.at[q, me_s, kept(q)],
            sends["third"], third_recv.at[q], ((me_t + shifts[q]) % n_tile, me_c, h),
        )

    def early_copy(h, k):
        return remote(
            partial.at[h, k, split, pl.ds(0, half)], early.at[h, k],
            sends["early"], early_recv.at[k], ((me_t + shifts[split]) % n_tile, me_c, me_s),
        )

    def send_early(k):
        for h in range(2):
            early_copy(h, k).start()

    def wait_early(k):
        all_of(early.at[:, k], sends["early"], early_recv.at[k]).wait_recv()

    loads[2].wait()
    cell = cell_ref[...]
    row, col = cell // WS, cell % WS
    position[...] = (
        (row // 4) * block + (row % 2) * (2 * quarter) + (col % 2) * quarter
        + ((row % 4) // 2) * half_cols + col // 2
    )
    loads[0].wait()
    wait_near(barrier)
    weight_copy(flip_x).start()
    weight_copy(flip_y).start()
    relay(0)
    loads[1].wait()
    columns = jnp.transpose(column_ref[...].astype(f32))
    loads[3].wait()

    def mask_rows(pair):
        for i in range(rows // 128):
            tiles = jnp.broadcast_to(columns[:, i:i + 1], (128, width)).astype(bf16)
            taken = values_ref[i * 128:(i + 1) * 128, :]
            for u in range(2):
                wanted = ((me_t + shifts[2 * pair + u]) % n_tile).astype(f32).astype(bf16)
                masked[pair][i * 128:(i + 1) * 128, u * width:(u + 1) * width] = jnp.where(
                    tiles == wanted, taken, jnp.zeros_like(taken)
                )

    ids = lax.broadcasted_iota(jnp.int32, (block, rows), 0).astype(bf16)

    def mark(k):
        for h in range(2):
            j = (diagonal, near[h], far[h], me_c)[k]
            offset = (position[...] - (h * n_chan + j) * block).astype(bf16)
            onehot[k][h * block:(h + 1) * block] = jnp.where(
                ids == offset, jnp.ones((), bf16), jnp.zeros((), bf16)
            )

    def grid_block(k, pair):
        sums = [
            jnp.dot(
                onehot[k][h * block:(h + 1) * block], masked[pair][...],
                preferred_element_type=f32,
            )
            for h in range(2)
        ]
        for h in range(2):
            for u in range(2):
                partial[h, k, 2 * pair + u] = sums[h][:, u * width:(u + 1) * width].astype(bf16)

    def send_first(k, q):
        if q == own:
            wait_early(k)
        for h in range(2):
            if q == own:
                partial[h, k, q, 0:half] = (
                    partial[h, k, q, 0:half].astype(f32) + early[h, k].astype(f32)
                ).astype(bf16)
            first_copy(h, k, q).start()

    def combined(h, k, q, arrived):
        total = partial[h, k, q, kept(q)].astype(f32)
        for ref in arrived:
            total = total + ref[kept(q)].astype(f32)
        if q == own:
            total = jnp.concatenate(
                [total[:half] + early[h, k].astype(f32), total[half:]], axis=0
            )
        return total.astype(bf16)

    def send_second(q):
        all_of(first.at[:, 0, q, kept(q)], sends["first"], first_recv.at[0, q]).wait_recv()
        if q == own:
            wait_early(2)
        for h in range(2):
            second_src[h, q, kept(q)] = combined(h, 2, q, (first.at[h, 0, q],))
            second_copy(h, q).start()

    def send_third(q):
        all_of(first.at[:, 1, q, kept(q)], sends["first"], first_recv.at[1, q]).wait_recv()
        all_of(second.at[:, q, kept(q)], sends["second"], second_recv.at[q]).wait_recv()
        if q == own:
            wait_early(3)
        for h in range(2):
            third_src[h, q, kept(q)] = combined(h, 3, q, (first.at[h, 1, q], second.at[h, q]))
            if q != own:
                third_copy(h, q).start()
        if q == own:
            third_copy_own.start()

    third_copy_own = remote(
        third_src.at[other, own], third.at[own, me_s], sends["third"], third_recv.at[own],
        (me_t, me_c, other),
    )

    mask_rows(0)
    mark(0)
    grid_block(0, 0)
    send_first(0, 0)
    send_first(0, 1)
    relay(1)
    mark(1)
    grid_block(1, 0)
    send_first(1, 0)
    send_first(1, 1)
    relay(2)
    send_early(0)
    send_early(1)
    mark(2)
    grid_block(2, 0)
    send_early(2)
    send_second(0)
    mark(3)
    mask_rows(1)
    grid_block(3, 0)
    send_early(3)
    send_second(1)
    relay(3)
    grid_block(0, 1)
    send_first(0, 2)
    grid_block(1, 1)
    send_first(1, 2)
    weight_copy(diagonal).start()
    send_third(0)
    send_third(1)
    grid_block(2, 1)
    loads[4].wait()
    pos = position[...]
    inner = pos % block
    code = (tile_ref[...] * n_chan + (pos // block) % n_chan) * 4
    code = code + (pos // (block * n_chan)) * 2 + inner // 128
    code_ids = lax.broadcasted_iota(jnp.int32, (n_tile * n_chan * 4, rows), 0)
    lane_ids = lax.broadcasted_iota(jnp.int32, (128, rows), 0)
    counts = lax.dot_general(
        (code_ids == code).astype(bf16), (lane_ids == inner % 128).astype(bf16),
        (((1,), (1,)), ((), ())), preferred_element_type=f32,
    )
    count_src[...] = counts.reshape(n_tile * n_chan * n_core, 2, 128)
    relay(4)
    for offset in offsets:
        count_copy(*offset).start()
    send_second(2)
    send_first(0, 3)
    send_first(1, 3)
    grid_block(3, 1)
    all_of(weights.at[0, :, 0:2], sends["weight"], recvs["weight"]).wait_recv()
    pass_copy(flip_x).start()
    pass_copy(flip_y).start()
    send_third(2)
    send_second(3)

    here = (me_t * n_core + me_s) * n_chan + me_c
    count = n_tile * n_core * n_chan
    hidden_all[0] = jnp.zeros((half_cols, 128), bf16)
    hidden_all[count + 1] = jnp.zeros((half_cols, 128), bf16)
    loads[5].wait()
    loads[6].wait()
    taps9 = depth_ref[...].astype(f32)
    taps9 = jnp.concatenate([taps9, taps9], axis=1)

    all_of(weights.at[0, :, 0], sends["weight"], recvs["cross"]).wait_recv()
    pass_copy(diagonal).start()
    send_third(own)

    all_of(count_in.at[0:len(offsets)], sends["count"], recvs["count"]).wait_recv()
    mine = count_src[here_index(me_t, me_c, me_s, n_chan, n_core)]
    theirs = jnp.zeros(mine.shape, f32)
    for i in range(n_tile * n_chan):
        if i:
            mine = mine + count_in[i]
        theirs = theirs + count_in[n_tile * n_chan + i]

    for q in range(own):
        all_of(third.at[q, :, kept(q)], sends["third"], third_recv.at[q]).wait_recv()
    third_copy_own.wait_recv()
    for slot, counted in ((me_s, mine), (other, theirs)):
        summed = third[0, slot].astype(f32) + third[2, slot].astype(f32)
        summed = jnp.concatenate(
            [summed[:half], summed[half:] + third[split, slot, half:].astype(f32)], axis=0
        )
        if slot is me_s:
            summed = summed + third_src[me_s, own].astype(f32)
        else:
            summed = summed + third[own, slot].astype(f32)
        divisor = jnp.maximum(counted, 1.0)
        for u in range(block // 128):
            each = jnp.transpose(jnp.broadcast_to(divisor[u:u + 1, :], (128, 128)))
            means[slot, u * 128:(u + 1) * 128] = (summed[u * 128:(u + 1) * 128] / each).astype(bf16)

    all_of(weights.at[0, :, 0:n_chan - 1], sends["pass"], recvs["pass"]).wait_recv()
    lanes = weights.shape[3]
    encoded = jnp.zeros((quarter, n_chan * lanes), f32)
    for a in range(2):
        for b in range(2):
            at_row = (2 * a + b) * quarter
            fields = jnp.concatenate(
                [means[s, at_row:at_row + quarter] for s in range(n_core)], axis=1
            )
            encoded = encoded + lax.dot_general(
                fields, weights[a, b].reshape(n_chan * lanes, n_core * width),
                (((1,), (1,)), ((), ())), preferred_element_type=f32,
            )
    hidden = jax.nn.gelu(encoded)
    lane = lax.broadcasted_iota(jnp.int32, (half_cols, 128), 1)
    for g in range(n_chan // 2):
        upper = hidden[:half_cols, g * 128:(g + 1) * 128]
        lower = hidden[half_cols:, g * 128:(g + 1) * 128]
        hidden_src[2 * g] = jnp.where(lane < 64, upper, pltpu.roll(lower, 64, 1)).astype(bf16)
        hidden_src[2 * g + 1] = jnp.where(lane < 64, pltpu.roll(upper, 64, 1), lower).astype(bf16)

    edge = 1 - ((me_c + 1) % n_chan) // 2

    def hidden_copy(a, b):
        to = at(a, b, 0)
        return remote(
            hidden_src.at[to[1]], hidden_all.at[here + 1], sends["hidden"],
            hidden_recv.at[edge], to,
        )

    for a in (2, 1, 3, 0):
        for b in range(n_chan):
            if a or b:
                hidden_copy(a, b).start()

    def swap_copy(t, j):
        here = hidden_all.at[(t * n_core + me_s) * n_chan + j + 1]
        return remote(here, here, sends["swap"], recvs["swap"], (me_t, me_c, other))

    hidden_all[here + 1] = hidden_src[me_c]
    most = pl.ds(0, block - half // n_tile)
    all_of(first.at[:, :, :, most], sends["first"], first_recv.at[0, 0]).wait_send()
    all_of(second.at[:, :, most], sends["second"], second_recv.at[0]).wait_send()
    all_of(third.at[0:own], sends["third"], third_recv.at[0]).wait_send()
    all_of(early, sends["early"], early_recv.at[0]).wait_send()
    all_of(weights.at[0, :, 0:n_chan - 1], sends["weight"], recvs["weight"]).wait_send()
    all_of(weights.at[0, :, 0:n_chan - 1], sends["pass"], recvs["pass"]).wait_send()
    all_of(count_in.at[0:len(offsets)], sends["count"], recvs["count"]).wait_send()
    every = n_tile * n_chan // 2

    def wait_hidden(kind):
        @pl.when(edge == kind)
        def _():
            all_of(
                hidden_all.at[0:every - 1], sends["hidden"], hidden_recv.at[kind]
            ).wait_recv()

        @pl.when(edge != kind)
        def _():
            all_of(hidden_all.at[0:every], sends["hidden"], hidden_recv.at[kind]).wait_recv()

    wait_hidden(1)
    for t in range(n_tile):
        for j in (0, n_chan - 1):
            swap_copy(t, j).start()
    wait_hidden(0)
    all_of(hidden_all.at[0:every], sends["swap"], recvs["swap"]).wait_recv()
    line = lax.broadcasted_iota(jnp.int32, (half_cols, 128), 0)
    for t in range(n_tile):
        j = jnp.int32(0)
        for i in range(n_chan):
            j = jnp.where(owners_ref[t, i] == me_t, i, j)
        at_piece = (t * n_core + me_s) * n_chan + j + 1
        total = jnp.zeros((half_cols, 128), f32)
        for p in range(3):
            field = hidden_all[at_piece + p - 1].astype(f32)
            before = jnp.where(line >= 2, pltpu.roll(field, 2, 0), 0.0)
            after = jnp.where(line < half_cols - 2, pltpu.roll(field, half_cols - 2, 0), 0.0)
            for q, shifted in enumerate((before, field, after)):
                total = total + shifted * taps9[3 * p + q:3 * p + q + 1, :]
            if p == 1:
                middle = field
        latent = middle + total
        out_ref[t, 0:half_cols] = latent[:, :64].astype(bf16)
        out_ref[t, half_cols:] = latent[:, 64:].astype(bf16)
    all_of(hidden_all.at[0:2 * every - 1], sends["hidden"], hidden_recv.at[0]).wait_send()
    all_of(hidden_all.at[0:every], sends["swap"], recvs["swap"]).wait_send()


def here_index(t, c, s, n_chan, n_core):
    return (t * n_chan + c) * n_core + s


SENDS = ("first", "second", "third", "weight", "pass", "count", "hidden", "early", "swap")
RECVS = ("weight", "cross", "pass", "count", "swap")
RELAYS = 4


def fused(observed_values, observed_tile, observed_cell, patch_weight, depth_weight, owners):
    f32, bf16, i32 = jnp.float32, jnp.bfloat16, jnp.int32
    n_tile, n_chan, n_core = (lax.axis_size(a) for a in ("tile", "chan", "tm"))
    values = observed_values[0]
    rows, width = values.shape
    depth_in, lanes = patch_weight.shape[1:]
    turned = jnp.swapaxes(patch_weight, 1, 2).reshape(2, 2, lanes, depth_in)
    block = HS * WS // (n_core * n_chan)
    cells = block // 4
    dma, vmem = pltpu.SemaphoreType.DMA, pltpu.VMEM
    pieces = n_tile * n_core * n_chan
    out = pl.pallas_call(
        fused_kernel,
        out_shape=vmem((n_tile, cells, lanes), bf16),
        in_specs=[pl.BlockSpec(memory_space=pl.ANY)] * 7,
        out_specs=pl.BlockSpec(memory_space=pltpu.VMEM),
        scratch_shapes=[
            vmem((rows, width), bf16),
            vmem((rows // 128, 128), i32),
            vmem((1, rows), i32),
            vmem((1, rows), i32),
            vmem(depth_weight.shape, bf16),
            pltpu.SMEM(owners.shape, i32),
            *[vmem((rows, 2 * width), bf16)] * 2,
            *[vmem((2 * block, rows), bf16)] * 4,
            vmem((1, rows), i32),
            vmem((2, 4, n_tile, block, width), bf16),
            vmem((2, 2, n_tile, block, width), bf16),
            vmem((2, n_tile, block, width), bf16),
            vmem((2, n_tile, block, width), bf16),
            vmem((2, n_tile, block, width), bf16),
            vmem((n_tile, 2, block, width), bf16),
            vmem((2, 4, block // 2, width), bf16),
            vmem((pieces, 2, 128), f32),
            vmem((pieces, 2, 128), f32),
            vmem((2, 2, n_chan, lanes, depth_in), bf16),
            vmem((2, block, width), bf16),
            vmem((n_chan, cells // 2, 128), bf16),
            vmem((pieces + 2, cells // 2, 128), bf16),
            dma((7,)), dma((len(SENDS),)), dma((len(RECVS),)),
            dma((2, n_tile)), dma((n_tile,)), dma((n_tile,)), dma((4,)), dma((2,)),
            pltpu.SemaphoreType.REGULAR((RELAYS,)),
        ],
        compiler_params=pltpu.CompilerParams(
            collective_id=0, has_side_effects=True, vmem_limit_bytes=56 * 2**20
        ),
    )(
        values, observed_tile.reshape(rows // 128, 128), observed_tile.reshape(1, rows),
        observed_cell, turned, depth_weight, owners,
    )
    return out.reshape(1, 1, n_tile, cells, lanes)


def fits(mesh):
    tile, chan, tm = (mesh.shape[a] for a in ("tile", "chan", "tm"))
    return tile == 4 and chan == 4 and tm == 2


def solution(mesh):
    placed = (
        P("tm", ("tile", "chan"), None),
        P("tm", ("tile", "chan"), None),
        P("tm", ("tile", "chan")),
        P(None, None, "chan"),
        P(None, "chan"),
        P(),
    )
    return jax.shard_map(
        fused if fits(mesh) else local,
        mesh=mesh,
        in_specs=placed,
        out_specs=P("tile", "tm", None, None, "chan"),
        check_vma=False,
    )
```

```python
import functools
import jax
import jax.numpy as jnp
from jax import lax
from jax.experimental import pallas as pl
from jax.experimental.pallas import tpu as pltpu
from jax.sharding import PartitionSpec as P

V = 128
HS = 32
WS = 64


def padded(x, sides, width):
    for axis, dim in sides:
        devices, length = (lax.axis_size(axis), x.shape[dim])
        up = [(i, (i + 1) % devices) for i in range(devices - 1)]
        down = [(j, i) for i, j in up]
        last = lax.slice_in_dim(x, length - width, length, axis=dim)
        first = lax.slice_in_dim(x, 0, width, axis=dim)
        before = lax.ppermute(last, axis, up)
        after = lax.ppermute(first, axis, down)
        x = jnp.concatenate([before, x, after], axis=dim)
    return x


def pack_rows(values, destination, placed, tile_count, capacity):
    match = (destination[:, None] == lax.iota(jnp.int32, tile_count)[None, :]).astype(jnp.int32)
    earlier = jnp.cumsum(match, axis=0) - match
    position = jnp.sum(earlier * match, axis=1)
    slot_index = destination * capacity + position
    width = values.shape[1]
    sent_values = jnp.zeros((tile_count * capacity, width), jnp.bfloat16).at[slot_index].set(values)
    sent_cells = jnp.full((tile_count * capacity,), -1, jnp.int32).at[slot_index].set(placed)
    return (
        sent_values.reshape(tile_count, capacity, width),
        sent_cells.reshape(tile_count, capacity),
    )


def grid_block(arrived_values, arrived_cells, first_cell):
    cell_ids = first_cell + lax.iota(jnp.int32, 128)
    matches = cell_ids[:, None] == arrived_cells[None, :]
    totals = jnp.dot(
        matches.astype(jnp.bfloat16), arrived_values, preferred_element_type=jnp.float32
    )
    counts = jnp.sum(matches.astype(jnp.float32), axis=1)
    return (totals, counts)


def patch_rows(field, weight, row_start, row_count):
    slab = lax.dynamic_slice_in_dim(field, 2 * row_start, 2 * row_count, 0)
    depth_in = field.shape[2]
    result = jnp.zeros((row_count * (field.shape[1] // 2), weight.shape[2]), jnp.float32)
    for tap_row in range(2):
        for tap_col in range(2):
            window = slab[tap_row::2, tap_col::2, :].reshape(-1, depth_in)
            result = result + jnp.dot(
                window, weight[tap_row * 2 + tap_col], preferred_element_type=jnp.float32
            )
    return result.reshape(row_count, field.shape[1] // 2, weight.shape[2])


def local(observed_values, observed_tile, observed_cell, patch_weight, depth_weight, owners):
    tile_count = lax.axis_size("tile")
    slot_count = lax.axis_size("tm")
    values = observed_values[0]
    capacity = 2 * values.shape[0] // tile_count
    sent_values, sent_cells = pack_rows(
        values, observed_tile[0, :, 0], observed_cell[0], tile_count, capacity
    )
    arrived = (
        lax.all_to_all(sent_values, "tile", split_axis=0, concat_axis=0, tiled=True),
        lax.all_to_all(sent_cells, "tile", split_axis=0, concat_axis=0, tiled=True),
    )
    arrived_values = arrived[0].reshape(-1, V)
    arrived_cells = arrived[1].reshape(-1)
    cell_count = HS * WS
    firsts = jnp.arange(cell_count // 128, dtype=jnp.int32) * 128
    totals, counts = lax.map(
        lambda first_cell: grid_block(arrived_values, arrived_cells, first_cell), firsts
    )
    totals = totals.reshape(cell_count, V)
    counts = counts.reshape(cell_count)
    totals, counts = (
        lax.psum(totals.astype(jnp.bfloat16), "chan").astype(jnp.float32),
        lax.psum(counts.astype(jnp.bfloat16), "chan").astype(jnp.float32),
    )
    means = (totals / jnp.maximum(counts, 1.0)[:, None]).astype(jnp.bfloat16)
    means = means.reshape(HS, WS, V)
    out_rows = HS // (2 * slot_count)
    half_cols = WS // 2
    stacked = lax.all_gather(means, "tm", axis=2, tiled=True)
    encoded = patch_rows(stacked, patch_weight, lax.axis_index("tm") * out_rows, out_rows)
    hidden = jax.nn.gelu(encoded).astype(jnp.bfloat16)
    rimmed = padded(hidden, ((("tile", "tm"), 0),), 2)
    widened = jnp.pad(rimmed, ((0, 0), (2, 2), (0, 0))).astype(jnp.float32)
    depth = jnp.zeros(hidden.shape, jnp.float32)
    for tap_row in range(3):
        for tap_col in range(3):
            shifted = widened[
                2 * tap_row : 2 * tap_row + out_rows, 2 * tap_col : 2 * tap_col + half_cols, :
            ]
            depth = depth + shifted * depth_weight[tap_row * 3 + tap_col].astype(jnp.float32)
    latent = (hidden.astype(jnp.float32) + depth).astype(jnp.bfloat16)
    channels = latent.shape[2]
    pieces = latent.reshape(tile_count, -1, channels)
    own_row = lax.dynamic_index_in_dim(owners, lax.axis_index("tile"), 0, keepdims=False)
    order = lax.iota(jnp.int32, tile_count)
    chosen = jnp.sum(
        order[None, :] * (own_row[None, :] == order[:, None]).astype(jnp.int32), axis=1
    )
    outgoing = pieces[chosen]
    received = lax.all_to_all(outgoing, "tile", split_axis=0, concat_axis=0, tiled=True)
    return received.reshape(1, 1, tile_count, -1, channels)


def fused_kernel(
    values_hbm, column_hbm, tile_hbm, cell_hbm, weight_hbm, depth_hbm, owners_hbm, out_ref,
    values_ref, column_ref, tile_ref, cell_ref, depth_ref, owners_ref,
    masked_a, masked_b, onehot_a, onehot_b, onehot_c, onehot_d, position, partial, first, second_src, second, third_src, third, early,
    count_src, count_in, weights, means, hidden_src, hidden_all,
    load_sems, send_sems, recv_sems, first_recv, second_recv, third_recv,
    early_recv, hidden_recv, relays,
):
    f32, bf16 = jnp.float32, jnp.bfloat16
    n_tile, n_chan, n_core = (lax.axis_size(a) for a in ("tile", "chan", "tm"))
    me_t, me_c, me_s = (lax.axis_index(a) for a in ("tile", "chan", "tm"))
    rows, width = values_ref.shape
    block = partial.shape[3]
    quarter = block // 4
    half_cols = WS // 2
    flip_x = me_c + 1 - 2 * (me_c % 2)
    flip_y = (me_c + 2) % 4
    diagonal = 3 - me_c
    near = (flip_x, flip_y)
    far = (flip_y, flip_x)
    other = 1 - me_s
    masked = (masked_a, masked_b)
    onehot = (onehot_a, onehot_b, onehot_c, onehot_d)
    shifts = (2, 3, 1, 0)
    half = early.shape[2]
    split = 1
    own = n_tile - 1
    sends = {n: send_sems.at[i] for i, n in enumerate(SENDS)}
    recvs = {n: recv_sems.at[i] for i, n in enumerate(RECVS)}

    def remote(source, target, send, recv, device):
        return pltpu.make_async_remote_copy(
            src_ref=source, dst_ref=target, send_sem=send, recv_sem=recv,
            device_id=device, device_id_type=pl.DeviceIdType.MESH,
        )

    def signal(sem, device):
        pl.semaphore_signal(sem, inc=1, device_id=device, device_id_type=pl.DeviceIdType.MESH)

    def all_of(ref, send, recv):
        return remote(ref, ref, send, recv, (me_t, me_c, other))

    offsets = [
        (a, b, c) for a in range(n_tile) for b in range(n_chan) for c in range(n_core)
    ][1:]

    def at(a, b, c):
        return ((me_t + a) % n_tile, (me_c + b) % n_chan, (me_s + c) % n_core)

    loads = [
        pltpu.make_async_copy(source, target, load_sems.at[i])
        for i, (source, target) in enumerate((
            (weight_hbm, weights.at[:, :, me_c]), (column_hbm, column_ref), (cell_hbm, cell_ref),
            (values_hbm, values_ref), (tile_hbm, tile_ref), (depth_hbm, depth_ref),
            (owners_hbm, owners_ref),
        ))
    ]
    for i in (2, 0, 1, 3, 4, 5, 6):
        loads[i].start()

    def signal_near(sem):
        for o in range(1, n_chan):
            signal(sem, (me_t, (me_c + o) % n_chan, me_s))
        signal(sem, (me_t, me_c, other))

        @pl.when(me_t > 0)
        def _():
            signal(sem, (me_t - 1, me_c, me_s))

        @pl.when(me_t < n_tile - 1)
        def _():
            signal(sem, (me_t + 1, me_c, me_s))

    def wait_near(sem):
        inner_tile = jnp.where((me_t > 0) & (me_t < n_tile - 1), 1, 0)
        pl.semaphore_wait(sem, n_chan + 1 + inner_tile)

    def relay(i):
        if i:
            wait_near(relays.at[i - 1])
        if i < RELAYS:
            signal_near(relays.at[i])

    barrier = pltpu.get_barrier_semaphore()
    signal_near(barrier)

    def weight_copy(to):
        here = weights.at[me_s, :, me_c]
        recv = recvs["cross" if to is diagonal else "weight"]
        return remote(here, here, sends["weight"], recv, (me_t, to, me_s))

    def pass_copy(of):
        here = weights.at[me_s, :, of]
        return remote(here, here, sends["pass"], recvs["pass"], (me_t, me_c, other))

    def count_copy(a, b, c):
        to = at(a, b, c)
        return remote(
            count_src.at[(to[0] * n_chan + to[1]) * n_core + to[2]],
            count_in.at[(c * n_tile + a) * n_chan + b],
            sends["count"], recvs["count"], to,
        )

    def kept(q):
        return pl.ds(half, block - half) if q == split else pl.ds(0, block)

    def first_copy(h, k, q):
        return remote(
            partial.at[h, k, q, kept(q)], first.at[h, k, q, kept(q)],
            sends["first"], first_recv.at[k, q], (me_t, near[h], me_s),
        )

    def second_copy(h, q):
        return remote(
            second_src.at[h, q, kept(q)], second.at[h, q, kept(q)],
            sends["second"], second_recv.at[q], (me_t, far[h], me_s),
        )

    def third_copy(h, q):
        return remote(
            third_src.at[h, q, kept(q)], third.at[q, me_s, kept(q)],
            sends[("third", "rest", "last")[q]], third_recv.at[q], ((me_t + shifts[q]) % n_tile, me_c, h),
        )

    def early_copy(h, k):
        return remote(
            partial.at[h, k, split, pl.ds(0, half)], early.at[h, k],
            sends["early"], early_recv.at[k], ((me_t + shifts[split]) % n_tile, me_c, me_s),
        )

    def send_early(k):
        for h in range(2):
            early_copy(h, k).start()

    def wait_early(k):
        all_of(early.at[:, k], sends["early"], early_recv.at[k]).wait_recv()

    loads[2].wait()
    cell = cell_ref[...]
    row, col = cell // WS, cell % WS
    position[...] = (
        (row // 4) * block + (row % 2) * (2 * quarter) + (col % 2) * quarter
        + ((row % 4) // 2) * half_cols + col // 2
    )
    loads[0].wait()
    wait_near(barrier)
    weight_copy(flip_x).start()
    weight_copy(flip_y).start()
    relay(0)
    loads[1].wait()
    columns = jnp.transpose(column_ref[...].astype(f32))
    loads[3].wait()

    def mask_rows(pair):
        for i in range(rows // 128):
            tiles = jnp.broadcast_to(columns[:, i:i + 1], (128, width)).astype(bf16)
            taken = values_ref[i * 128:(i + 1) * 128, :]
            for u in range(2):
                wanted = ((me_t + shifts[2 * pair + u]) % n_tile).astype(f32).astype(bf16)
                masked[pair][i * 128:(i + 1) * 128, u * width:(u + 1) * width] = jnp.where(
                    tiles == wanted, taken, jnp.zeros_like(taken)
                )

    ids = lax.broadcasted_iota(jnp.int32, (block, rows), 0).astype(bf16)

    def mark(k):
        for h in range(2):
            j = (diagonal, near[h], far[h], me_c)[k]
            offset = (position[...] - (h * n_chan + j) * block).astype(bf16)
            onehot[k][h * block:(h + 1) * block] = jnp.where(
                ids == offset, jnp.ones((), bf16), jnp.zeros((), bf16)
            )

    def grid_block(k, pair):
        sums = [
            jnp.dot(
                onehot[k][h * block:(h + 1) * block], masked[pair][...],
                preferred_element_type=f32,
            )
            for h in range(2)
        ]
        for h in range(2):
            for u in range(2):
                partial[h, k, 2 * pair + u] = sums[h][:, u * width:(u + 1) * width].astype(bf16)

    def send_first(k, q):
        if q == own:
            wait_early(k)
        for h in range(2):
            if q == own:
                partial[h, k, q, 0:half] = (
                    partial[h, k, q, 0:half].astype(f32) + early[h, k].astype(f32)
                ).astype(bf16)
            first_copy(h, k, q).start()

    def combined(h, k, q, arrived):
        total = partial[h, k, q, kept(q)].astype(f32)
        for ref in arrived:
            total = total + ref[kept(q)].astype(f32)
        if q == own:
            total = jnp.concatenate(
                [total[:half] + early[h, k].astype(f32), total[half:]], axis=0
            )
        return total.astype(bf16)

    def send_second(q):
        all_of(first.at[:, 0, q, kept(q)], sends["first"], first_recv.at[0, q]).wait_recv()
        if q == own:
            wait_early(2)
        for h in range(2):
            second_src[h, q, kept(q)] = combined(h, 2, q, (first.at[h, 0, q],))
            second_copy(h, q).start()

    def send_third(q):
        all_of(first.at[:, 1, q, kept(q)], sends["first"], first_recv.at[1, q]).wait_recv()
        all_of(second.at[:, q, kept(q)], sends["second"], second_recv.at[q]).wait_recv()
        if q == own:
            wait_early(3)
        for h in range(2):
            third_src[h, q, kept(q)] = combined(h, 3, q, (first.at[h, 1, q], second.at[h, q]))
            if q != own:
                third_copy(h, q).start()
        if q == own:
            third_copy_own.start()

    third_copy_own = remote(
        third_src.at[other, own], third.at[own, me_s], sends["own"], third_recv.at[own],
        (me_t, me_c, other),
    )

    mask_rows(0)
    mark(0)
    grid_block(0, 0)
    send_first(0, 0)
    send_first(0, 1)
    relay(1)
    mark(1)
    grid_block(1, 0)
    send_first(1, 0)
    send_first(1, 1)
    relay(2)
    send_early(0)
    send_early(1)
    mark(2)
    grid_block(2, 0)
    send_early(2)
    send_second(0)
    mark(3)
    mask_rows(1)
    grid_block(3, 0)
    send_early(3)
    send_second(1)
    relay(3)
    grid_block(0, 1)
    send_first(0, 2)
    grid_block(1, 1)
    send_first(1, 2)
    weight_copy(diagonal).start()
    send_third(0)
    send_third(1)
    grid_block(2, 1)
    loads[4].wait()
    pos = position[...]
    inner = pos % block
    code = (tile_ref[...] * n_chan + (pos // block) % n_chan) * 4
    code = code + (pos // (block * n_chan)) * 2 + inner // 128
    code_ids = lax.broadcasted_iota(jnp.int32, (n_tile * n_chan * 4, rows), 0)
    lane_ids = lax.broadcasted_iota(jnp.int32, (128, rows), 0)
    counts = lax.dot_general(
        (code_ids == code).astype(bf16), (lane_ids == inner % 128).astype(bf16),
        (((1,), (1,)), ((), ())), preferred_element_type=f32,
    )
    count_src[...] = counts.reshape(n_tile * n_chan * n_core, 2, 128)
    relay(4)
    for offset in offsets:
        count_copy(*offset).start()
    send_second(2)
    send_first(0, 3)
    send_first(1, 3)
    grid_block(3, 1)
    all_of(weights.at[0, :, 0:2], sends["weight"], recvs["weight"]).wait_recv()
    pass_copy(flip_x).start()
    pass_copy(flip_y).start()
    send_third(2)
    send_second(3)

    here = (me_t * n_core + me_s) * n_chan + me_c
    count = n_tile * n_core * n_chan
    hidden_all[0] = jnp.zeros((half_cols, 128), bf16)
    hidden_all[count + 1] = jnp.zeros((half_cols, 128), bf16)
    loads[5].wait()
    loads[6].wait()
    taps9 = depth_ref[...].astype(f32)
    taps9 = jnp.concatenate([taps9, taps9], axis=1)

    all_of(weights.at[0, :, 0], sends["weight"], recvs["cross"]).wait_recv()
    pass_copy(diagonal).start()
    send_third(own)

    all_of(count_in.at[0:len(offsets)], sends["count"], recvs["count"]).wait_recv()
    mine = count_src[here_index(me_t, me_c, me_s, n_chan, n_core)]
    theirs = jnp.zeros(mine.shape, f32)
    for i in range(n_tile * n_chan):
        if i:
            mine = mine + count_in[i]
        theirs = theirs + count_in[n_tile * n_chan + i]

    for q in range(own):
        all_of(third.at[q, :, kept(q)], sends["third"], third_recv.at[q]).wait_recv()
    third_copy_own.wait_recv()
    for slot, counted in ((me_s, mine), (other, theirs)):
        summed = third[0, slot].astype(f32) + third[2, slot].astype(f32)
        summed = jnp.concatenate(
            [summed[:half], summed[half:] + third[split, slot, half:].astype(f32)], axis=0
        )
        if slot is me_s:
            summed = summed + third_src[me_s, own].astype(f32)
        else:
            summed = summed + third[own, slot].astype(f32)
        divisor = jnp.maximum(counted, 1.0)
        for u in range(block // 128):
            each = jnp.transpose(jnp.broadcast_to(divisor[u:u + 1, :], (128, 128)))
            means[slot, u * 128:(u + 1) * 128] = (summed[u * 128:(u + 1) * 128] / each).astype(bf16)

    all_of(weights.at[0, :, 0:n_chan - 1], sends["pass"], recvs["pass"]).wait_recv()
    lanes = weights.shape[3]
    encoded = jnp.zeros((quarter, n_chan * lanes), f32)
    for a in range(2):
        for b in range(2):
            at_row = (2 * a + b) * quarter
            fields = jnp.concatenate(
                [means[s, at_row:at_row + quarter] for s in range(n_core)], axis=1
            )
            encoded = encoded + lax.dot_general(
                fields, weights[a, b].reshape(n_chan * lanes, n_core * width),
                (((1,), (1,)), ((), ())), preferred_element_type=f32,
            )
    hidden = jax.nn.gelu(encoded)
    lane = lax.broadcasted_iota(jnp.int32, (half_cols, 128), 1)
    for g in range(n_chan // 2):
        upper = hidden[:half_cols, g * 128:(g + 1) * 128]
        lower = hidden[half_cols:, g * 128:(g + 1) * 128]
        hidden_src[2 * g] = jnp.where(lane < 64, upper, pltpu.roll(lower, 64, 1)).astype(bf16)
        hidden_src[2 * g + 1] = jnp.where(lane < 64, pltpu.roll(upper, 64, 1), lower).astype(bf16)

    edge = 1 - ((me_c + 1) % n_chan) // 2

    def hidden_copy(a, b):
        to = at(a, b, 0)
        return remote(
            hidden_src.at[to[1]], hidden_all.at[here + 1], sends["hidden"],
            hidden_recv.at[edge], to,
        )

    for a in (2, 1, 3, 0):
        for b in range(n_chan):
            if a or b:
                hidden_copy(a, b).start()

    def swap_copy(t, j):
        here = hidden_all.at[(t * n_core + me_s) * n_chan + j + 1]
        return remote(here, here, sends["swap"], recvs["swap"], (me_t, me_c, other))

    hidden_all[here + 1] = hidden_src[me_c]
    most = pl.ds(0, block - half // n_tile)
    all_of(first.at[:, :, :, most], sends["first"], first_recv.at[0, 0]).wait_send()
    all_of(second.at[:, :, most], sends["second"], second_recv.at[0]).wait_send()
    for q, name in enumerate(("third", "rest", "last")):
        all_of(third.at[q, :, kept(q)], sends[name], third_recv.at[q]).wait_send()
    third_copy_own.wait_send()
    all_of(early, sends["early"], early_recv.at[0]).wait_send()
    all_of(weights.at[0, :, 0:n_chan - 1], sends["weight"], recvs["weight"]).wait_send()
    all_of(weights.at[0, :, 0:n_chan - 1], sends["pass"], recvs["pass"]).wait_send()
    all_of(count_in.at[0:len(offsets)], sends["count"], recvs["count"]).wait_send()
    every = n_tile * n_chan // 2

    def wait_hidden(kind):
        @pl.when(edge == kind)
        def _():
            all_of(
                hidden_all.at[0:every - 1], sends["hidden"], hidden_recv.at[kind]
            ).wait_recv()

        @pl.when(edge != kind)
        def _():
            all_of(hidden_all.at[0:every], sends["hidden"], hidden_recv.at[kind]).wait_recv()

    wait_hidden(1)
    for t in range(n_tile):
        for j in (0, n_chan - 1):
            swap_copy(t, j).start()
    wait_hidden(0)
    all_of(hidden_all.at[0:every], sends["swap"], recvs["swap"]).wait_recv()
    line = lax.broadcasted_iota(jnp.int32, (half_cols, 128), 0)
    for t in range(n_tile):
        j = jnp.int32(0)
        for i in range(n_chan):
            j = jnp.where(owners_ref[t, i] == me_t, i, j)
        at_piece = (t * n_core + me_s) * n_chan + j + 1
        total = jnp.zeros((half_cols, 128), f32)
        for p in range(3):
            field = hidden_all[at_piece + p - 1].astype(f32)
            before = jnp.where(line >= 2, pltpu.roll(field, 2, 0), 0.0)
            after = jnp.where(line < half_cols - 2, pltpu.roll(field, half_cols - 2, 0), 0.0)
            for q, shifted in enumerate((before, field, after)):
                total = total + shifted * taps9[3 * p + q:3 * p + q + 1, :]
            if p == 1:
                middle = field
        latent = middle + total
        out_ref[t, 0:half_cols] = latent[:, :64].astype(bf16)
        out_ref[t, half_cols:] = latent[:, 64:].astype(bf16)
    all_of(hidden_all.at[0:2 * every - 1], sends["hidden"], hidden_recv.at[0]).wait_send()
    all_of(hidden_all.at[0:every], sends["swap"], recvs["swap"]).wait_send()


def here_index(t, c, s, n_chan, n_core):
    return (t * n_chan + c) * n_core + s


SENDS = ("first", "second", "third", "weight", "pass", "count", "hidden", "early", "swap", "rest", "last", "own")
RECVS = ("weight", "cross", "pass", "count", "swap")
RELAYS = 4


def fused(observed_values, observed_tile, observed_cell, patch_weight, depth_weight, owners):
    f32, bf16, i32 = jnp.float32, jnp.bfloat16, jnp.int32
    n_tile, n_chan, n_core = (lax.axis_size(a) for a in ("tile", "chan", "tm"))
    values = observed_values[0]
    rows, width = values.shape
    depth_in, lanes = patch_weight.shape[1:]
    turned = jnp.swapaxes(patch_weight, 1, 2).reshape(2, 2, lanes, depth_in)
    block = HS * WS // (n_core * n_chan)
    cells = block // 4
    dma, vmem = pltpu.SemaphoreType.DMA, pltpu.VMEM
    pieces = n_tile * n_core * n_chan
    out = pl.pallas_call(
        fused_kernel,
        out_shape=vmem((n_tile, cells, lanes), bf16),
        in_specs=[pl.BlockSpec(memory_space=pl.ANY)] * 7,
        out_specs=pl.BlockSpec(memory_space=pltpu.VMEM),
        scratch_shapes=[
            vmem((rows, width), bf16),
            vmem((rows // 128, 128), i32),
            vmem((1, rows), i32),
            vmem((1, rows), i32),
            vmem(depth_weight.shape, bf16),
            pltpu.SMEM(owners.shape, i32),
            *[vmem((rows, 2 * width), bf16)] * 2,
            *[vmem((2 * block, rows), bf16)] * 4,
            vmem((1, rows), i32),
            vmem((2, 4, n_tile, block, width), bf16),
            vmem((2, 2, n_tile, block, width), bf16),
            vmem((2, n_tile, block, width), bf16),
            vmem((2, n_tile, block, width), bf16),
            vmem((2, n_tile, block, width), bf16),
            vmem((n_tile, 2, block, width), bf16),
            vmem((2, 4, block * 3 // 4, width), bf16),
            vmem((pieces, 2, 128), f32),
            vmem((pieces, 2, 128), f32),
            vmem((2, 2, n_chan, lanes, depth_in), bf16),
            vmem((2, block, width), bf16),
            vmem((n_chan, cells // 2, 128), bf16),
            vmem((pieces + 2, cells // 2, 128), bf16),
            dma((7,)), dma((len(SENDS),)), dma((len(RECVS),)),
            dma((2, n_tile)), dma((n_tile,)), dma((n_tile,)), dma((4,)), dma((2,)),
            pltpu.SemaphoreType.REGULAR((RELAYS,)),
        ],
        compiler_params=pltpu.CompilerParams(
            collective_id=0, has_side_effects=True, vmem_limit_bytes=56 * 2**20
        ),
    )(
        values, observed_tile.reshape(rows // 128, 128), observed_tile.reshape(1, rows),
        observed_cell, turned, depth_weight, owners,
    )
    return out.reshape(1, 1, n_tile, cells, lanes)


def fits(mesh):
    tile, chan, tm = (mesh.shape[a] for a in ("tile", "chan", "tm"))
    return tile == 4 and chan == 4 and tm == 2


def solution(mesh):
    placed = (
        P("tm", ("tile", "chan"), None),
        P("tm", ("tile", "chan"), None),
        P("tm", ("tile", "chan")),
        P(None, None, "chan"),
        P(None, "chan"),
        P(),
    )
    return jax.shard_map(
        fused if fits(mesh) else local,
        mesh=mesh,
        in_specs=placed,
        out_specs=P("tile", "tm", None, None, "chan"),
        check_vma=False,
    )
```
